128 devices in a mesh: dp: 16 (over x_lo, z, core), mp: 8 (over x_hi, y).
Axes of the slice: x: 4 (x_hi: 2, x_lo: 2; x = x_hi * 2 + x_lo), y: 4, z: 4, core: 2. Of those that a mesh axis runs over, the one named last changes fastest.
Arguments:
- tokens: bfloat16 [8192, 1280], P('dp'), may hold values from -6 to 6
- norm_gain: float32 [1280], replicated, may hold values from 0.25 to 1.75
- widen_weight: bfloat16 [1280, 5120], P(None, 'mp'), may hold values from -0.15625 to 0.15625
- narrow_weight: bfloat16 [5120, 1280], P('mp'), may hold values from -0.078125 to 0.078125
- final_gain: float32 [1280], replicated, may hold values from 0.25 to 1.75
- adaptor_in: bfloat16 [3, 1280, 1280], P(None, None, 'mp'), may hold values from -0.15625 to 0.15625
- head_dino: bfloat16 [1280, 1536], P('mp'), may hold values from -0.15625 to 0.15625
- head_siglip: bfloat16 [1280, 1152], P('mp'), may hold values from -0.15625 to 0.15625
- head_sam: bfloat16 [1280, 1280], P('mp'), may hold values from -0.15625 to 0.15625
- teacher_dino: bfloat16 [2, 8192, 1536], P(None, 'dp', 'mp'), may hold values from -6 to 6
- teacher_siglip: bfloat16 [2, 8192, 1152], P(None, 'dp', 'mp'), may hold values from -6 to 6
- teacher_sam: bfloat16 [2, 8192, 1280], P(None, 'dp', 'mp'), may hold values from -6 to 6
- step_lags: int32 [3], replicated, may hold values from 1 to 2, as said below
- owner_slot: int32 [256], replicated, may hold values from 0 to 255, as said below
Outputs:
- grad_widen: float32 [5120, 1280], P('mp', 'dp')
- grad_narrow: float32 [5120, 1280], P('mp', 'dp')
- grad_adaptor: float32 [3, 1280, 1280], P(None, 'dp', 'mp')
- grad_dino: float32 [1280, 1536], P('mp', 'dp')
- grad_siglip: float32 [1280, 1152], P('mp', 'dp')
- grad_sam: float32 [1280, 1280], P('mp', 'dp')
The draws below stay inside these ranges and needn't reach their ends.
Inputs may be any that keep to these rules, and one draw needn't show every extreme that they name: owner_slot is a permutation; of the 16 images in each aligned block of 16 images, exactly 1 have slots in each aligned block of 16 slots. `step_lags`: the three lags are not all equal.
All inputs are finite; a program needn't handle non-finite values.
Results may differ from the reference program's by a relative error of at most 0.02.
Values may be sent and summed in bfloat16 or wider, within the bound.
A program may use at most 128 MiB of HBM per device.

```python
import jax
import jax.numpy as jnp
from jax import lax

D = 1280
FF = 5120
HID = 1280
C_DINO = 1536
C_SIGLIP = 1152
C_SAM = 1280
PATCH = 32
IMG_DP = 16
IMAGES = 256
TOKENS = 8192


def draw_owner_slot(key, part):
    groups = IMAGES // IMG_DP
    share = IMG_DP // groups
    key_images, key_slots = jax.random.split(jax.random.fold_in(key, 7))
    image_perm = jax.vmap(lambda sub: jax.random.permutation(sub, IMG_DP))(jax.random.split(key_images, groups))
    slot_perm = jax.vmap(lambda sub: jax.random.permutation(sub, IMG_DP))(jax.random.split(key_slots, groups))
    source = jnp.arange(groups, dtype=jnp.int32)[:, None, None]
    target = jnp.arange(groups, dtype=jnp.int32)[None, :, None]
    within = jnp.arange(share, dtype=jnp.int32)[None, None, :]
    image = source * IMG_DP + image_perm[source, target * share + within]
    slot = target * IMG_DP + slot_perm[target, source * share + within]
    return jnp.zeros((IMAGES,), jnp.int32).at[image.reshape(-1)].set(slot.reshape(-1).astype(jnp.int32))


def draw_step_lags(key, part):
    key_free, key_order = jax.random.split(jax.random.fold_in(key, 11))
    free = jax.random.randint(key_free, (1,), 1, 3, dtype=jnp.int32)
    values = jnp.concatenate([jnp.array([1, 2], dtype=jnp.int32), free.astype(jnp.int32)])
    return jax.random.permutation(key_order, values).astype(jnp.int32)


def spiked(drawn, stream_key, source, target, shards_of, factor):
    owner, partner = [(jnp.arange(drawn.shape[position]) // (drawn.shape[position] // shards_of)).reshape([-1 if axis == position else 1 for axis in range(drawn.ndim)]) for position in (source, target)]
    chosen = jax.random.permutation(stream_key, shards_of)[partner]
    strong = (owner == chosen) | (owner == (partner + shards_of // 2) % shards_of)
    return jnp.where(strong, factor * drawn, drawn)


def steps_of(key, extent, pieces, low, high):
    level, own = 1.0, jax.random.fold_in(key, 6)
    for dim, blocks in pieces:
        draws = jnp.exp(jax.random.uniform(jax.random.fold_in(own, dim), (blocks,), jnp.float32, low / len(pieces), high / len(pieces)))
        level = level * jnp.repeat(draws, extent[dim] // blocks).reshape([-1 if axis == dim else 1 for axis in range(len(extent))])
    return level


def gaussian(key, shape, deviation, reach, cuts=(), kind=jnp.bfloat16):
    values = deviation * jax.random.normal(key, shape, jnp.float32)
    if cuts:
        values = values * steps_of(key, shape, cuts, -0.22, 0.18)
    return jnp.clip(values, -reach, reach).astype(kind)


def heavy_noise(stream_key, shape, scale, bound, shards, heavy, kind=jnp.bfloat16):
    entries = scale * jax.random.normal(stream_key, shape, jnp.float32)
    if shards:
        entries = entries * steps_of(stream_key, shape, shards, -0.22, 0.18)
    return jnp.clip(spiked(entries, jax.random.fold_in(stream_key, 3), *heavy), -bound, bound).astype(kind)


def setup_inputs(seed: int = 0) -> dict:
    keys = jax.random.split(jax.random.key(seed), 15)
    tokens = heavy_noise(keys[0], (TOKENS, D), 1.0, 6.0, ((0, 16),), (0, 1, 16, 2.0))
    norm_gain = jnp.clip(1.0 + 0.15 * jax.random.normal(keys[1], (D,), jnp.float32), 0.25, 1.75)
    widen_weight = gaussian(keys[2], (D, FF), D ** -0.5, 0.15625, ((1, 8),))
    narrow_weight = gaussian(keys[3], (FF, D), FF ** -0.5, 0.078125, ((0, 8),))
    final_gain = jnp.clip(1.0 + 0.15 * jax.random.normal(keys[4], (D,), jnp.float32), 0.25, 1.75)
    adaptor_in = gaussian(keys[5], (3, D, HID), D ** -0.5, 0.15625, ((2, 8),))
    head_dino = gaussian(keys[6], (HID, C_DINO), HID ** -0.5, 0.15625, ((0, 8),))
    head_siglip = gaussian(keys[7], (HID, C_SIGLIP), HID ** -0.5, 0.15625, ((0, 8),))
    head_sam = gaussian(keys[8], (HID, C_SAM), HID ** -0.5, 0.15625, ((0, 8),))
    teacher_dino = gaussian(keys[9], (2, TOKENS, C_DINO), 1.0, 6.0, ((1, 16), (2, 8)))
    teacher_siglip = gaussian(keys[10], (2, TOKENS, C_SIGLIP), 1.0, 6.0, ((1, 16), (2, 8)))
    teacher_sam = gaussian(keys[11], (2, TOKENS, C_SAM), 1.0, 6.0, ((1, 16), (2, 8)))
    step_lags = draw_step_lags(jax.random.fold_in(keys[14], 71), 0)
    owner_slot = draw_owner_slot(jax.random.fold_in(keys[14], 71), 0)
    return {"tokens": tokens, "norm_gain": norm_gain, "widen_weight": widen_weight, "narrow_weight": narrow_weight, "final_gain": final_gain, "adaptor_in": adaptor_in, "head_dino": head_dino, "head_siglip": head_siglip, "head_sam": head_sam, "teacher_dino": teacher_dino, "teacher_siglip": teacher_siglip, "teacher_sam": teacher_sam, "step_lags": step_lags, "owner_slot": owner_slot}


slope_coef = 0.7978845608028654
cubic_coef = 0.044715

def smooth(value):
    return 0.5 * value * (1.0 + jnp.tanh(slope_coef * (value + cubic_coef * value * value * value)))

def smooth_slope(value):
    tangent = jnp.tanh(slope_coef * (value + cubic_coef * value * value * value))
    return 0.5 * (1.0 + tangent) + 0.5 * value * (1.0 - tangent * tangent) * slope_coef * (1.0 + 3.0 * cubic_coef * value * value)

def normalize(value, gain):
    centre = value - lax.optimization_barrier(jnp.mean(value, axis=-1, keepdims=True))
    inverse = lax.rsqrt(lax.optimization_barrier(jnp.mean(centre * centre, axis=-1, keepdims=True)) + 1e-06)
    normal = centre * inverse
    return (normal * gain, normal, inverse)

def normalize_back(upstream, gain, normal, inverse):
    scaled = upstream * gain
    return inverse * (scaled - lax.optimization_barrier(jnp.mean(scaled, axis=-1, keepdims=True)) - normal * lax.optimization_barrier(jnp.mean(scaled * normal, axis=-1, keepdims=True)))

def finish(product, square_student, square_target, student, target):
    joint = lax.rsqrt(square_student * square_target)
    cosine = product * joint
    slope = cosine[:, None] * student / square_student[:, None] - target * joint[:, None]
    return (cosine, slope)

def reference(tokens, norm_gain, widen_weight, narrow_weight, final_gain, adaptor_in, head_dino, head_siglip, head_sam, teacher_dino, teacher_siglip, teacher_sam, step_lags, owner_slot):
    heads = (head_dino, head_siglip, head_sam)
    teachers = (teacher_dino, teacher_siglip, teacher_sam)
    placing = jnp.argsort(owner_slot).astype(jnp.int32)
    first, normal_one, inverse_one = normalize(tokens.astype(jnp.float32), norm_gain)
    first = first.astype(jnp.bfloat16)
    widened = jnp.dot(first, widen_weight, preferred_element_type=jnp.float32)
    active = smooth(widened).astype(jnp.bfloat16)
    hidden = tokens.astype(jnp.float32) + jnp.dot(active, narrow_weight, preferred_element_type=jnp.float32)
    final, normal_two, inverse_two = normalize(hidden, final_gain)
    final = final.astype(jnp.bfloat16)
    upstream = jnp.zeros(hidden.shape, jnp.float32)
    head_grads = []
    adaptor_grads = []
    for index in range(3):
        before = jnp.dot(final, adaptor_in[index], preferred_element_type=jnp.float32)
        lifted = smooth(before).astype(jnp.bfloat16)
        student = jnp.dot(lifted, heads[index], preferred_element_type=jnp.float32)
        stale = lax.dynamic_index_in_dim(teachers[index], step_lags[index] - 1, 0, keepdims=False)
        width = stale.shape[-1]
        target = jnp.take(stale.reshape(IMAGES, PATCH, width), placing, axis=0).reshape(TOKENS, width).astype(jnp.float32)
        product = lax.optimization_barrier(jnp.sum(student * target, axis=-1))
        square_student = lax.optimization_barrier(jnp.sum(student * student, axis=-1)) + 1e-06
        square_target = lax.optimization_barrier(jnp.sum(target * target, axis=-1)) + 1e-06
        cosine, slope = finish(product, square_student, square_target, student, target)
        slope = slope.astype(jnp.bfloat16)
        head_grads.append(jnp.dot(lifted.T, slope, preferred_element_type=jnp.float32))
        back = jnp.dot(slope, heads[index].T, preferred_element_type=jnp.float32)
        inner = (back * smooth_slope(before)).astype(jnp.bfloat16)
        adaptor_grads.append(jnp.dot(final.T, inner, preferred_element_type=jnp.float32))
        upstream = upstream + jnp.dot(inner, adaptor_in[index].T, preferred_element_type=jnp.float32)
    through = normalize_back(upstream, final_gain, normal_two, inverse_two).astype(jnp.bfloat16)
    grad_narrow = jnp.dot(active.T, through, preferred_element_type=jnp.float32)
    back_two = jnp.dot(through, narrow_weight.T, preferred_element_type=jnp.float32)
    inner_two = (back_two * smooth_slope(widened)).astype(jnp.bfloat16)
    grad_widen = jnp.dot(inner_two.T, first, preferred_element_type=jnp.float32)
    return (grad_widen, grad_narrow, jnp.stack(adaptor_grads), head_grads[0], head_grads[1], head_grads[2])
```

```python
import jax
import jax.numpy as jnp
from jax import lax
from jax.experimental import pallas as pl
from jax.experimental.pallas import tpu as pltpu
from jax.sharding import PartitionSpec as P

F32, BF16 = jnp.float32, jnp.bfloat16
MESH = pl.DeviceIdType.MESH

R, D, FB, HB = 512, 1280, 640, 160
DP, MP, PATCH = 16, 8, 32
WIDTHS = (1536, 1152, 1280)
CB = tuple(w // MP for w in WIDTHS)
PB = tuple(w // DP for w in WIDTHS)
BASE = (0, 1536, 2688)
OFF = (0, 192, 336)
HOFF = (0, 96, 176)
CH, CBS = 3968, 496
BLK = R // MP
DB = D // DP

slope_coef = 0.7978845608028654
cubic_coef = 0.044715


def smooth(value):
    return 0.5 * value * (1.0 + jnp.tanh(slope_coef * (value + cubic_coef * value * value * value)))


def smooth_slope(value):
    square = value * value
    tangent = jnp.tanh(slope_coef * (value + cubic_coef * value * square))
    return 0.5 * (1.0 + tangent) + 0.5 * value * (1.0 - tangent * tangent) * slope_coef * (
        1.0 + 3.0 * cubic_coef * square
    )


def nn(a, b):
    return lax.dot_general(a, b, (((1,), (0,)), ((), ())), preferred_element_type=F32)


def nt(a, b):
    return lax.dot_general(a, b, (((1,), (1,)), ((), ())), preferred_element_type=F32)


def eye(n):
    return (
        lax.broadcasted_iota(jnp.int32, (n, n), 0) == lax.broadcasted_iota(jnp.int32, (n, n), 1)
    ).astype(F32).astype(BF16)


def flipped(block):
    return nt(eye(block.shape[1]), block).astype(BF16)


def remote(src, dst, send, recv, where):
    return pltpu.make_async_remote_copy(
        src_ref=src, dst_ref=dst, send_sem=send, recv_sem=recv, device_id=where, device_id_type=MESH
    )


def aligned(value, n):
    return pl.multiple_of(value, n)


def kernel(
    lags, slots, tok, ng, ww, nw, fg, ai, h0, h1, h2, t0, t1, t2,
    out_w, out_n, out_a, out_h,
    first, wide, active, part, rs1, final, normal, inverse,
    headt, before, lift, sp, rs2, stu, tsend, trecv, tgt, stats, statr,
    slo, inner, part2, rs3, thr, finalt,
    hf32, hsend, hcore, hmid, hrecv, asend, acore, amid, arecv,
    nsend, ncore, nmid, nrecv, wsend, wcore, wmid, wrecv,
    row_s, row_r, tea_s, tea_r, stu_s, stu_r, sta_s, sta_r, slo_s, slo_r,
    cor_s, cor_r, dp_s, dp_r,
):
    d = lax.axis_index("dp")
    m = lax.axis_index("mp")
    core = lax.rem(d, 2)
    half = d // 2
    heads = (h0, h1, h2)
    teachers = (t0, t1, t2)
    partner = half * 2 + (1 - core)

    def mate(i):
        return lax.rem(m + i, MP)

    def greet(i, _):
        pl.semaphore_signal(barrier, inc=1, device_id={"mp": mate(i)}, device_id_type=MESH)
        return _

    def greet_dp(i, _):
        pl.semaphore_signal(barrier, inc=1, device_id={"dp": lax.rem(d + i, DP)}, device_id_type=MESH)
        return _

    barrier = pltpu.get_barrier_semaphore()
    lax.fori_loop(1, MP, greet, 0)
    lax.fori_loop(1, DP, greet_dp, 0)
    pl.semaphore_wait(barrier, MP - 1 + DP - 1)

    def forward(i, _):
        q = lax.rem(m // 2 + 1 + i, 4)
        rows = pl.ds(aligned(q * 128, 128), 128)
        value = tok[rows, :].astype(F32)
        centre = value - jnp.mean(value, axis=-1, keepdims=True)
        inv = lax.rsqrt(jnp.mean(centre * centre, axis=-1, keepdims=True) + 1e-06)
        first[rows, :] = (centre * inv * ng[...]).astype(BF16)
        w = nn(first[rows, :], ww[...])
        wide[rows, :] = w
        active[rows, :] = smooth(w).astype(BF16)
        part[rows, :] = nn(active[rows, :], nw[...]).astype(BF16)
        for k in range(2):
            p = q * 2 + k

            @pl.when(p != m)
            def _send():
                mine = part.at[pl.ds(aligned(p * BLK, BLK), BLK)]
                remote(mine, rs1.at[m], row_s.at[0, p], row_r.at[0, m], {"mp": p}).start()

        return _

    lax.fori_loop(0, 4, forward, 0)

    def slopes_of(ref, n):
        def body(i, _):
            rows = pl.ds(aligned(i * 32, 32), 32)
            ref[rows, :] = smooth_slope(ref[rows, :])
            return _

        lax.fori_loop(0, n // 32, body, 0)

    def grid(shape, dim):
        return lax.broadcasted_iota(jnp.int32, shape, dim)

    def ones_where(condition):
        return condition.astype(F32).astype(BF16)

    slot = slots[...].reshape(1, DP * DP)
    spread_out = ones_where(grid((DP * DP, R), 0) == d * DP + grid((DP * DP, R), 1) // PATCH)
    own_slot = nn(jnp.broadcast_to(slot, (16, DP * DP)).astype(F32).astype(BF16), spread_out)[0:1]
    goes = own_slot.astype(jnp.int32) // DP
    same_patch = lax.rem(grid((R, R), 0), PATCH) == lax.rem(grid((R, R), 1), PATCH)
    chosen = ones_where((goes == grid((R, R), 0) // PATCH) & same_patch)
    for t in range(3):
        late = (lags[t] - 1).astype(F32)
        stale = teachers[t][0].astype(F32) * (1.0 - late) + teachers[t][1].astype(F32) * late
        tsend[:, 256 * t : 256 * t + CB[t]] = nt(chosen, stale.astype(BF16)).astype(BF16)

    def images_of(j):
        return pl.ds(aligned(j * PATCH, PATCH), PATCH)

    def teach(i, _):
        j = lax.rem(d + i, DP)
        remote(tsend.at[images_of(j)], trecv.at[images_of(d)], tea_s.at[j], tea_r.at[d], {"dp": j}).start()
        return _

    lax.fori_loop(1, DP, teach, 0)
    trecv[images_of(d), :] = tsend[images_of(d), :]

    slopes_of(wide, R)
    for t in range(3):
        def head_block(i, _, t=t):
            at = aligned(i * 128, 128)
            headt[pl.ds(aligned(BASE[t] + at, 128), 128), :] = flipped(heads[t][:, pl.ds(at, 128)])
            return _

        lax.fori_loop(0, WIDTHS[t] // 128, head_block, 0)

    own_rows = pl.ds(aligned(m * BLK, BLK), BLK)

    def gathered(buffer, which, received):
        total = buffer[own_rows, :].astype(F32)
        for i in range(1, MP):
            p = mate(i)
            remote(received.at[p], received.at[p], row_s.at[which, p], row_r.at[which, p], {"mp": p}).wait_recv()
            total = total + received[p].astype(F32)
        return total

    def spread(buffer, which):
        def body(i, _):
            p = mate(i)
            remote(buffer.at[own_rows], buffer.at[own_rows], row_s.at[which, p], row_r.at[which, m], {"mp": p}).start()
            return _

        lax.fori_loop(1, MP, body, 0)

    def arrived(buffer, which):
        def body(i, _):
            p = mate(i)
            there = buffer.at[pl.ds(aligned(p * BLK, BLK), BLK)]
            remote(there, there, row_s.at[which, p], row_r.at[which, p], {"mp": p}).wait_recv()
            return _

        lax.fori_loop(1, MP, body, 0)

    hidden = tok[own_rows, :].astype(F32) + gathered(part, 0, rs1)
    centre = hidden - jnp.mean(hidden, axis=-1, keepdims=True)
    inv = lax.rsqrt(jnp.mean(centre * centre, axis=-1, keepdims=True) + 1e-06)
    normal[...] = centre * inv
    inverse[...] = jnp.broadcast_to(inv, (BLK, 128))
    final[own_rows, :] = (normal[...] * fg[...]).astype(BF16)
    spread(final, 1)

    def landed(i, _):
        j = lax.rem(d + i, DP)
        remote(tsend.at[images_of(j)], trecv.at[images_of(j)], tea_s.at[j], tea_r.at[j], {"dp": j}).wait_recv()
        return _

    lax.fori_loop(1, DP, landed, 0)

    holds = ones_where(slot == d * DP + grid((R, DP * DP), 0) // PATCH)
    group = ones_where(grid((R, DP * DP), 1) // DP == grid((R, DP * DP), 0) // PATCH)
    placing = jnp.where(same_patch, nt(group, holds), 0.0).astype(BF16)
    for t in range(3):
        block = flipped(trecv[:, 256 * t : 256 * t + CB[t]])
        tgt[OFF[t] : OFF[t] + CB[t], :] = nn(block, placing).astype(BF16)

    arrived(final, 1)

    for t in range(3):
        units = slice(t * HB, (t + 1) * HB)
        b = nt(ai[t], final[...])
        before[units, :] = b
        lift[units, :] = smooth(b).astype(BF16)

        def student(i, _, t=t, units=units):
            p = mate(i)
            rows = pl.ds(aligned(BASE[t] + p * CB[t], 16), CB[t])
            sp[rows, :] = nn(headt[rows, :], lift[units, :]).astype(BF16)

            @pl.when(p != m)
            def _send():
                there = rs2.at[m, OFF[t] : OFF[t] + CB[t]]
                remote(sp.at[rows], there, stu_s.at[t, p], stu_r.at[t, m], {"mp": p}).start()

            return _

        lax.fori_loop(1, MP + 1, student, 0)

    slopes_of(before, 3 * HB)

    def final_block(i, _):
        at = aligned(i * 128, 128)
        finalt[pl.ds(at, 128), :] = flipped(final[:, pl.ds(at, 128)])
        return _

    lax.fori_loop(0, D // 128, final_block, 0)

    def gather_student(t):
        mine = slice(OFF[t], OFF[t] + CB[t])
        stu[mine, :] = sp[pl.ds(aligned(BASE[t] + m * CB[t], 16), CB[t]), :].astype(F32)

        def body(i, _):
            p = mate(i)
            here = rs2.at[p, mine]
            remote(here, here, stu_s.at[t, p], stu_r.at[t, p], {"mp": p}).wait_recv()
            stu[mine, :] += rs2[p, mine].astype(F32)
            return _

        lax.fori_loop(1, MP, body, 0)
        y = stu[mine, :]
        f = tgt[mine, :].astype(F32)
        stats[t, 0:1, :] = jnp.sum(y * f, axis=0, keepdims=True)
        stats[t, 1:2, :] = jnp.sum(y * y, axis=0, keepdims=True)
        stats[t, 2:3, :] = jnp.sum(f * f, axis=0, keepdims=True)
        stats[t, 3:8, :] = jnp.zeros((5, R), F32)

        def send(i, _):
            p = mate(i)
            remote(stats.at[t], statr.at[t, m], sta_s.at[t, p], sta_r.at[t, m], {"mp": p}).start()
            return _

        lax.fori_loop(1, MP, send, 0)

    def slope(t):
        mine = slice(OFF[t], OFF[t] + CB[t])
        total = stats[t]
        for i in range(1, MP):
            p = mate(i)
            remote(stats.at[t], statr.at[t, p], sta_s.at[t, p], sta_r.at[t, p], {"mp": p}).wait_recv()
            total = total + statr[t, p]
        square_student = total[1:2] + 1e-06
        joint = lax.rsqrt(square_student * (total[2:3] + 1e-06))
        scale = total[0:1] * joint / square_student
        rows = pl.ds(aligned(BASE[t] + m * CB[t], 16), CB[t])
        slo[rows, :] = (scale * stu[mine, :] - joint * tgt[mine, :].astype(F32)).astype(BF16)

        def send(i, _):
            p = mate(i)
            remote(slo.at[rows], slo.at[rows], slo_s.at[t, p], slo_r.at[t, m], {"mp": p}).start()
            return _

        lax.fori_loop(1, MP, send, 0)

    gather_student(0)
    gather_student(1)
    slope(0)
    gather_student(2)
    slope(1)
    slope(2)

    for t in range(3):
        def slopes_in(i, _, t=t):
            p = mate(i)
            there = slo.at[pl.ds(aligned(BASE[t] + p * CB[t], 16), CB[t])]
            remote(there, there, slo_s.at[t, p], slo_r.at[t, p], {"mp": p}).wait_recv()
            return _

        lax.fori_loop(1, MP, slopes_in, 0)
        units = slice(t * HB, (t + 1) * HB)
        back = nn(heads[t][...], slo[BASE[t] : BASE[t] + WIDTHS[t], :])
        inner[units, :] = (back * before[units, :]).astype(BF16)

    def up(i, _):
        q = lax.rem(m // 2 + 1 + i, 4)
        rows = pl.ds(aligned(q * 128, 128), 128)
        part2[rows, :] = nn(flipped(inner[:, rows]), ai[...].reshape(3 * HB, D)).astype(BF16)
        for k in range(2):
            p = q * 2 + k

            @pl.when(p != m)
            def _send():
                mine = part2.at[pl.ds(aligned(p * BLK, BLK), BLK)]
                remote(mine, rs3.at[m], row_s.at[2, p], row_r.at[2, m], {"mp": p}).start()

        return _

    lax.fori_loop(0, 4, up, 0)

    def to_partner(which, send, received):
        def body(k, _):
            j = k * 2 + (1 - core)
            remote(send.at[j], received.at[k], cor_s.at[which, k], cor_r.at[which, k], {"dp": partner}).start()
            return _

        lax.fori_loop(0, 8, body, 0)

    def onward(which, send, received, mid, last):
        def body(i, _):
            k = lax.rem(half + i, 8)
            remote(send.at[k], received.at[k], cor_s.at[which, k], cor_r.at[which, k], {"dp": partner}).wait_recv()
            mid[k] = (send[k * 2 + core].astype(F32) + received[k].astype(F32)).astype(BF16)

            @pl.when(k != half)
            def _send():
                remote(mid.at[k], last.at[half], dp_s.at[which, k], dp_r.at[which, half], {"dp": k * 2 + core}).start()

            return _

        lax.fori_loop(1, 9, body, 0)

    def reduced(which, mid, last, out):
        out[...] = mid[half].astype(F32)

        def body(i, _):
            k = lax.rem(half + i, 8)
            remote(mid.at[k], last.at[k], dp_s.at[which, k], dp_r.at[which, k], {"dp": k * 2 + core}).wait_recv()
            out[...] += last[k].astype(F32)
            return _

        lax.fori_loop(1, 8, body, 0)

    for t in range(3):
        def head_grad(i, _, t=t):
            at = aligned(i * 128, 128)
            rows = pl.ds(aligned(BASE[t] + at, 128), 128)
            hf32[pl.ds(at, 128), :] = nt(slo[rows, :], lift[t * HB : (t + 1) * HB, :])
            return _

        lax.fori_loop(0, WIDTHS[t] // 128, head_grad, 0)

        def head_piece(j, _, t=t):
            rows = pl.ds(aligned(j * PB[t], 8), PB[t])
            hsend[j, HOFF[t] : HOFF[t] + PB[t], :] = hf32[rows, :].astype(BF16)
            return _

        lax.fori_loop(0, DP, head_piece, 0)
    to_partner(0, hsend, hcore)

    def adaptor_grad(j, _):
        asend[j] = nt(finalt[pl.ds(aligned(j * DB, 16), DB), :], inner[...]).astype(BF16)
        return _

    lax.fori_loop(0, DP, adaptor_grad, 0)
    to_partner(1, asend, acore)
    onward(0, hsend, hcore, hmid, hrecv)
    onward(1, asend, acore, amid, arecv)

    upstream = gathered(part2, 2, rs3)
    scaled = upstream * fg[...]
    hat = normal[...]
    through = inverse[:, 0:1] * (
        scaled
        - jnp.mean(scaled, axis=-1, keepdims=True)
        - hat * jnp.mean(scaled * hat, axis=-1, keepdims=True)
    )
    thr[own_rows, :] = through.astype(BF16)
    spread(thr, 3)
    arrived(thr, 3)

    def flip_all(src):
        def body(i, _):
            at = aligned(i * 128, 128)
            finalt[pl.ds(at, 128), :] = flipped(src[:, pl.ds(at, 128)])
            return _

        lax.fori_loop(0, D // 128, body, 0)

    flip_all(thr)

    def narrow_grad(j, _):
        nsend[j] = nn(finalt[pl.ds(aligned(j * DB, 16), DB), :], active[...]).astype(BF16)
        return _

    lax.fori_loop(0, DP, narrow_grad, 0)
    to_partner(2, nsend, ncore)
    flip_all(first)

    def backward(i, _):
        rows = pl.ds(aligned(i * 128, 128), 128)
        active[rows, :] = (nt(thr[rows, :], nw[...]) * wide[rows, :]).astype(BF16)
        return _

    lax.fori_loop(0, 4, backward, 0)
    onward(2, nsend, ncore, nmid, nrecv)

    def widen_grad(j, _):
        wsend[j] = nn(finalt[pl.ds(aligned(j * DB, 16), DB), :], active[...]).astype(BF16)
        return _

    lax.fori_loop(0, DP, widen_grad, 0)
    to_partner(3, wsend, wcore)
    onward(3, wsend, wcore, wmid, wrecv)
    reduced(0, hmid, hrecv, out_h)
    reduced(1, amid, arecv, out_a)
    reduced(2, nmid, nrecv, out_n)
    reduced(3, wmid, wrecv, out_w)

    def sent_dp(i, _):
        j = lax.rem(d + i, DP)
        remote(tsend.at[images_of(j)], trecv.at[images_of(d)], tea_s.at[j], tea_r.at[d], {"dp": j}).wait_send()
        return _

    lax.fori_loop(1, DP, sent_dp, 0)

    def sent_mp(i, _):
        p = mate(i)
        where = {"mp": p}
        for which, (src, dst) in enumerate(((part, rs1), (final, rs1), (part2, rs3), (thr, rs3))):
            remote(src.at[own_rows], dst.at[m], row_s.at[which, p], row_r.at[which, m], where).wait_send()
        for t in range(3):
            rows = pl.ds(aligned(BASE[t] + p * CB[t], 16), CB[t])
            there = rs2.at[m, OFF[t] : OFF[t] + CB[t]]
            remote(sp.at[rows], there, stu_s.at[t, p], stu_r.at[t, m], where).wait_send()
            remote(stats.at[t], statr.at[t, m], sta_s.at[t, p], sta_r.at[t, m], where).wait_send()
            remote(slo.at[rows], slo.at[rows], slo_s.at[t, p], slo_r.at[t, m], where).wait_send()
        return _

    lax.fori_loop(1, MP, sent_mp, 0)
    reductions = (
        (hsend, hcore, hmid, hrecv),
        (asend, acore, amid, arecv),
        (nsend, ncore, nmid, nrecv),
        (wsend, wcore, wmid, wrecv),
    )

    def sent_core(k, _):
        for which, (send, received, mid, last) in enumerate(reductions):
            remote(send.at[k], received.at[k], cor_s.at[which, k], cor_r.at[which, k], {"dp": partner}).wait_send()
        return _

    lax.fori_loop(0, 8, sent_core, 0)

    def sent_chip(i, _):
        k = lax.rem(half + i, 8)
        for which, (send, received, mid, last) in enumerate(reductions):
            remote(mid.at[k], last.at[half], dp_s.at[which, k], dp_r.at[which, half], {"dp": k * 2 + core}).wait_send()
        return _

    lax.fori_loop(1, 8, sent_chip, 0)


def local(
    tokens, norm_gain, widen_weight, narrow_weight, final_gain, adaptor_in,
    head_dino, head_siglip, head_sam, teacher_dino, teacher_siglip, teacher_sam,
    step_lags, owner_slot,
):
    vmem = pl.BlockSpec(memory_space=pltpu.VMEM)

    def reduction(rows, columns):
        return [
            pltpu.VMEM((DP, rows, columns), BF16),
            pltpu.VMEM((8, rows, columns), BF16),
            pltpu.VMEM((8, rows, columns), BF16),
            pltpu.VMEM((8, rows, columns), BF16),
        ]

    dma = pltpu.SemaphoreType.DMA
    w, n, a, h = pl.pallas_call(
        kernel,
        out_shape=(
            jax.ShapeDtypeStruct((DB, FB), F32),
            jax.ShapeDtypeStruct((DB, FB), F32),
            jax.ShapeDtypeStruct((DB, 3 * HB), F32),
            jax.ShapeDtypeStruct((256, HB), F32),
        ),
        in_specs=[pl.BlockSpec(memory_space=pltpu.SMEM)] + [vmem] * 13,
        out_specs=(vmem,) * 4,
        scratch_shapes=[
            pltpu.VMEM((R, D), BF16),
            pltpu.VMEM((R, FB), F32),
            pltpu.VMEM((R, FB), BF16),
            pltpu.VMEM((R, D), BF16),
            pltpu.VMEM((MP, BLK, D), BF16),
            pltpu.VMEM((R, D), BF16),
            pltpu.VMEM((BLK, D), F32),
            pltpu.VMEM((BLK, 128), F32),
            pltpu.VMEM((CH, HB), BF16),
            pltpu.VMEM((3 * HB, R), F32),
            pltpu.VMEM((3 * HB, R), BF16),
            pltpu.VMEM((CH, R), BF16),
            pltpu.VMEM((MP, CBS, R), BF16),
            pltpu.VMEM((CBS, R), F32),
            pltpu.VMEM((R, 768), BF16),
            pltpu.VMEM((R, 768), BF16),
            pltpu.VMEM((CBS, R), BF16),
            pltpu.VMEM((3, 8, R), F32),
            pltpu.VMEM((3, MP, 8, R), F32),
            pltpu.VMEM((CH, R), BF16),
            pltpu.VMEM((3 * HB, R), BF16),
            pltpu.VMEM((R, D), BF16),
            pltpu.VMEM((MP, BLK, D), BF16),
            pltpu.VMEM((R, D), BF16),
            pltpu.VMEM((D, R), BF16),
            pltpu.VMEM((1536, HB), F32),
            *reduction(256, HB),
            *reduction(DB, 3 * HB),
            *reduction(DB, FB),
            *reduction(DB, FB),
            dma((4, MP)), dma((4, MP)),
            dma((DP,)), dma((DP,)),
            dma((3, MP)), dma((3, MP)),
            dma((3, MP)), dma((3, MP)),
            dma((3, MP)), dma((3, MP)),
            dma((4, 8)), dma((4, 8)),
            dma((4, 8)), dma((4, 8)),
        ],
        compiler_params=pltpu.CompilerParams(
            collective_id=0, has_side_effects=True, vmem_limit_bytes=66_000_000
        ),
        name="step",
    )(
        step_lags, owner_slot[None], tokens, norm_gain[None], widen_weight, narrow_weight, final_gain[None],
        adaptor_in.transpose(0, 2, 1), head_dino, head_siglip, head_sam,
        teacher_dino.transpose(0, 2, 1), teacher_siglip.transpose(0, 2, 1), teacher_sam.transpose(0, 2, 1),
    )
    return (
        w.T,
        n.T,
        a.reshape(DB, 3, HB).transpose(1, 0, 2),
        h[0:96].T,
        h[96:168].T,
        h[176:256].T,
    )


def solution(mesh):
    placed = (
        P("dp", None),
        P(),
        P(None, "mp"),
        P("mp", None),
        P(),
        P(None, None, "mp"),
        P("mp", None),
        P("mp", None),
        P("mp", None),
        P(None, "dp", "mp"),
        P(None, "dp", "mp"),
        P(None, "dp", "mp"),
        P(),
        P(),
    )
    return jax.shard_map(
        local,
        mesh=mesh,
        in_specs=placed,
        out_specs=(
            P("mp", "dp"),
            P("mp", "dp"),
            P(None, "dp", "mp"),
            P("mp", "dp"),
            P("mp", "dp"),
            P("mp", "dp"),
        ),
        check_vma=False,
    )
```

```python
import jax
import jax.numpy as jnp
from jax import lax
from jax.experimental import pallas as pl
from jax.experimental.pallas import tpu as pltpu
from jax.sharding import PartitionSpec as P

F32, BF16 = jnp.float32, jnp.bfloat16
MESH = pl.DeviceIdType.MESH

R, D, FB, HB = 512, 1280, 640, 160
DP, MP, PATCH = 16, 8, 32
WIDTHS = (1536, 1152, 1280)
CB = tuple(w // MP for w in WIDTHS)
PB = tuple(w // DP for w in WIDTHS)
BASE = (0, 1536, 2688)
OFF = (0, 192, 336)
HOFF = (0, 96, 176)
CH, CBS = 3968, 496
BLK = R // MP
DB = D // DP

slope_coef = 0.7978845608028654
cubic_coef = 0.044715


def smooth(value):
    return 0.5 * value * (1.0 + jnp.tanh(slope_coef * (value + cubic_coef * value * value * value)))


def smooth_slope(value):
    square = value * value
    tangent = jnp.tanh(slope_coef * (value + cubic_coef * value * square))
    return 0.5 * (1.0 + tangent) + 0.5 * value * (1.0 - tangent * tangent) * slope_coef * (
        1.0 + 3.0 * cubic_coef * square
    )


def nn(a, b):
    return lax.dot_general(a, b, (((1,), (0,)), ((), ())), preferred_element_type=F32)


def nt(a, b):
    return lax.dot_general(a, b, (((1,), (1,)), ((), ())), preferred_element_type=F32)


def eye(n):
    return (
        lax.broadcasted_iota(jnp.int32, (n, n), 0) == lax.broadcasted_iota(jnp.int32, (n, n), 1)
    ).astype(F32).astype(BF16)


def flipped(block):
    return nt(eye(block.shape[1]), block).astype(BF16)


def remote(src, dst, send, recv, where):
    return pltpu.make_async_remote_copy(
        src_ref=src, dst_ref=dst, send_sem=send, recv_sem=recv, device_id=where, device_id_type=MESH
    )


def aligned(value, n):
    return pl.multiple_of(value, n)


def kernel(
    lags, slots, ng, fg, *refs,
):
    outside, refs = refs[:10], refs[10:]
    outputs, inside, load_sem, refs = refs[:6], refs[6:16], refs[16], refs[17:]
    step(lags, slots, ng, fg, outside, load_sem, *inside, *outputs, *refs)


def step(
    lags, slots, ng, fg, outside, load_sem, tok, ww, nw, t0, t1, t2, ai, h0, h1, h2,
    out_w, out_n, out_a, out_d, out_g, out_s,
    first, wide, active, part, rs1, final, normal, inverse,
    headt, before, lift, sp, rs2, stu, tsend, trecv, tgt, stats, statr,
    slo, inner, part2, rs3, thr, finalt, firstt,
    hf32, hacc, aacc, hsend, hcore, hmid, hrecv, asend, acore, amid, arecv,
    nsend, ncore, nmid, nrecv, wsend, wcore, wmid, wrecv,
    row_s, row_r, tea_s, tea_r, stu_s, stu_r, sta_s, sta_r, slo_s, slo_r,
    cor_s, cor_r, dp_s, dp_r,
):
    d = lax.axis_index("dp")
    m = lax.axis_index("mp")
    core = lax.rem(d, 2)
    half = d // 2
    loads = [
        pltpu.make_async_copy(src, dst, load_sem.at[k])
        for k, (src, dst) in enumerate(zip(outside, (tok, ww, nw, t0, t1, t2, ai, h0, h1, h2)))
    ]
    heads = (h0, h1, h2)
    teachers = (t0, t1, t2)
    partner = half * 2 + (1 - core)

    def mate(i):
        return lax.rem(m + i, MP)

    def greet(i, _):
        pl.semaphore_signal(barrier, inc=1, device_id={"mp": mate(i)}, device_id_type=MESH)
        return _

    def greet_dp(i, _):
        pl.semaphore_signal(barrier, inc=1, device_id={"dp": lax.rem(d + i, DP)}, device_id_type=MESH)
        return _

    barrier = pltpu.get_barrier_semaphore()
    lax.fori_loop(1, MP, greet, 0)
    lax.fori_loop(1, DP, greet_dp, 0)
    for load in loads:
        load.start()
    loads[0].wait()

    def normalized(i, _):
        rows = pl.ds(aligned(i * 128, 128), 128)
        value = tok[rows, :].astype(F32)
        centre = value - jnp.mean(value, axis=-1, keepdims=True)
        inv = lax.rsqrt(jnp.mean(centre * centre, axis=-1, keepdims=True) + 1e-06)
        first[rows, :] = (centre * inv * ng[...]).astype(BF16)
        return _

    lax.fori_loop(0, 4, normalized, 0)
    loads[1].wait()
    loads[2].wait()
    pl.semaphore_wait(barrier, MP - 1 + DP - 1)

    def forward(i, _):
        q = lax.rem(m // 2 + 1 + i, 4)
        rows = pl.ds(aligned(q * 128, 128), 128)
        w = nn(first[rows, :], ww[...])
        wide[rows, :] = w
        active[rows, :] = smooth(w).astype(BF16)
        part[rows, :] = nn(active[rows, :], nw[...]).astype(BF16)
        for k in range(2):
            p = q * 2 + k

            @pl.when(p != m)
            def _send():
                mine = part.at[pl.ds(aligned(p * BLK, BLK), BLK)]
                remote(mine, rs1.at[m], row_s.at[0, p], row_r.at[0, m], {"mp": p}).start()

        return _

    lax.fori_loop(0, 4, forward, 0)

    def slopes_of(ref, n):
        def body(i, _):
            rows = pl.ds(aligned(i * 32, 32), 32)
            ref[rows, :] = smooth_slope(ref[rows, :])
            return _

        lax.fori_loop(0, n // 32, body, 0)

    def grid(shape, dim):
        return lax.broadcasted_iota(jnp.int32, shape, dim)

    def ones_where(condition):
        return condition.astype(F32).astype(BF16)

    for load in loads[3:]:
        load.wait()
    slot = slots[...].reshape(1, DP * DP)
    spread_out = ones_where(grid((DP * DP, R), 0) == d * DP + grid((DP * DP, R), 1) // PATCH)
    own_slot = nn(jnp.broadcast_to(slot, (16, DP * DP)).astype(F32).astype(BF16), spread_out)[0:1]
    goes = own_slot.astype(jnp.int32) // DP
    same_patch = lax.rem(grid((R, R), 0), PATCH) == lax.rem(grid((R, R), 1), PATCH)
    chosen = ones_where((goes == grid((R, R), 0) // PATCH) & same_patch)
    for t in range(3):
        late = (lags[t] - 1).astype(F32)
        stale = teachers[t][0].astype(F32) * (1.0 - late) + teachers[t][1].astype(F32) * late
        tsend[:, 256 * t : 256 * t + CB[t]] = nt(chosen, stale.astype(BF16)).astype(BF16)

    def images_of(j):
        return pl.ds(aligned(j * PATCH, PATCH), PATCH)

    def teach(i, _):
        j = lax.rem(d + i, DP)
        remote(tsend.at[images_of(j)], trecv.at[images_of(d)], tea_s.at[j], tea_r.at[d], {"dp": j}).start()
        return _

    lax.fori_loop(1, DP, teach, 0)
    trecv[images_of(d), :] = tsend[images_of(d), :]

    slopes_of(wide, R)
    for t in range(3):
        def head_block(i, _, t=t):
            at = aligned(i * 128, 128)
            headt[pl.ds(aligned(BASE[t] + at, 128), 128), :] = flipped(heads[t][:, pl.ds(at, 128)])
            return _

        lax.fori_loop(0, WIDTHS[t] // 128, head_block, 0)

    own_rows = pl.ds(aligned(m * BLK, BLK), BLK)

    def gathered(buffer, which, received):
        total = buffer[own_rows, :].astype(F32)
        for i in range(1, MP):
            p = mate(i)
            remote(received.at[p], received.at[p], row_s.at[which, p], row_r.at[which, p], {"mp": p}).wait_recv()
            total = total + received[p].astype(F32)
        return total

    def spread(buffer, which):
        def body(i, _):
            p = mate(i)
            remote(buffer.at[own_rows], buffer.at[own_rows], row_s.at[which, p], row_r.at[which, m], {"mp": p}).start()
            return _

        lax.fori_loop(1, MP, body, 0)

    def arrived(buffer, which):
        def body(i, _):
            p = mate(i)
            there = buffer.at[pl.ds(aligned(p * BLK, BLK), BLK)]
            remote(there, there, row_s.at[which, p], row_r.at[which, p], {"mp": p}).wait_recv()
            return _

        lax.fori_loop(1, MP, body, 0)

    hidden = tok[own_rows, :].astype(F32) + gathered(part, 0, rs1)
    centre = hidden - jnp.mean(hidden, axis=-1, keepdims=True)
    inv = lax.rsqrt(jnp.mean(centre * centre, axis=-1, keepdims=True) + 1e-06)
    normal[...] = centre * inv
    inverse[...] = jnp.broadcast_to(inv, (BLK, 128))
    final[own_rows, :] = (normal[...] * fg[...]).astype(BF16)
    spread(final, 1)

    def landed(i, _):
        j = lax.rem(d + i, DP)
        remote(tsend.at[images_of(j)], trecv.at[images_of(j)], tea_s.at[j], tea_r.at[j], {"dp": j}).wait_recv()
        return _

    lax.fori_loop(1, DP, landed, 0)

    holds = ones_where(slot == d * DP + grid((R, DP * DP), 0) // PATCH)
    group = ones_where(grid((R, DP * DP), 1) // DP == grid((R, DP * DP), 0) // PATCH)
    placing = jnp.where(same_patch, nt(group, holds), 0.0).astype(BF16)
    for t in range(3):
        block = flipped(trecv[:, 256 * t : 256 * t + CB[t]])
        tgt[OFF[t] : OFF[t] + CB[t], :] = nn(block, placing).astype(BF16)

    arrived(final, 1)

    for t in range(3):
        units = slice(t * HB, (t + 1) * HB)
        b = nt(ai[t], final[...])
        before[units, :] = b
        lift[units, :] = smooth(b).astype(BF16)

        def student(i, _, t=t, units=units):
            p = mate(i)
            rows = pl.ds(aligned(BASE[t] + p * CB[t], 16), CB[t])
            sp[rows, :] = nn(headt[rows, :], lift[units, :]).astype(BF16)

            @pl.when(p != m)
            def _send():
                there = rs2.at[m, OFF[t] : OFF[t] + CB[t]]
                remote(sp.at[rows], there, stu_s.at[t, p], stu_r.at[t, m], {"mp": p}).start()

            return _

        lax.fori_loop(1, MP + 1, student, 0)

    slopes_of(before, 3 * HB)

    def flip_all(src, dst):
        def body(i, _):
            at = aligned(i * 128, 128)
            dst[pl.ds(at, 128), :] = flipped(src[:, pl.ds(at, 128)])
            return _

        lax.fori_loop(0, D // 128, body, 0)

    flip_all(final, finalt)
    flip_all(first, firstt)

    def gather_student(t):
        mine = slice(OFF[t], OFF[t] + CB[t])
        stu[mine, :] = sp[pl.ds(aligned(BASE[t] + m * CB[t], 16), CB[t]), :].astype(F32)

        def body(i, _):
            p = mate(i)
            here = rs2.at[p, mine]
            remote(here, here, stu_s.at[t, p], stu_r.at[t, p], {"mp": p}).wait_recv()
            stu[mine, :] += rs2[p, mine].astype(F32)
            return _

        lax.fori_loop(1, MP, body, 0)
        y = stu[mine, :]
        f = tgt[mine, :].astype(F32)
        stats[t, 0:1, :] = jnp.sum(y * f, axis=0, keepdims=True)
        stats[t, 1:2, :] = jnp.sum(y * y, axis=0, keepdims=True)
        stats[t, 2:3, :] = jnp.sum(f * f, axis=0, keepdims=True)
        stats[t, 3:8, :] = jnp.zeros((5, R), F32)

        def send(i, _):
            p = mate(i)
            remote(stats.at[t], statr.at[t, m], sta_s.at[t, p], sta_r.at[t, m], {"mp": p}).start()
            return _

        lax.fori_loop(1, MP, send, 0)

    def slope(t):
        mine = slice(OFF[t], OFF[t] + CB[t])
        total = stats[t]
        for i in range(1, MP):
            p = mate(i)
            remote(stats.at[t], statr.at[t, p], sta_s.at[t, p], sta_r.at[t, p], {"mp": p}).wait_recv()
            total = total + statr[t, p]
        square_student = total[1:2] + 1e-06
        joint = lax.rsqrt(square_student * (total[2:3] + 1e-06))
        scale = total[0:1] * joint / square_student
        rows = pl.ds(aligned(BASE[t] + m * CB[t], 16), CB[t])
        slo[rows, :] = (scale * stu[mine, :] - joint * tgt[mine, :].astype(F32)).astype(BF16)

        pass_on(t, m, 0, place(pair, ring + 1))
        pass_on(t, m, 1, place(pair, ring + 3))
        pass_on(t, m, 2, place(1 - pair, ring))

    pair, ring = m // 4, lax.rem(m, 4)
    turn = (1, 3, 3)

    def place(a, b):
        return a * 4 + lax.rem(b, 4)

    def slope_copy(t, owner, k, to):
        block = slo.at[pl.ds(aligned(BASE[t] + owner * CB[t], 16), CB[t])]
        return remote(block, block, slo_s.at[t, k], slo_r.at[t, owner], {"mp": to})

    def pass_on(t, owner, k, to):
        slope_copy(t, owner, k, to).start()

    def got(t, owner):
        slope_copy(t, owner, 0, owner).wait_recv()

    def first_relay(t):
        owner = place(pair, ring + 4 - turn[t])
        got(t, owner)
        pass_on(t, owner, 3, place(pair, ring + turn[t]))
        owner = place(1 - pair, ring)
        got(t, owner)
        pass_on(t, owner, 4, place(pair, ring + turn[t]))
        pass_on(t, owner, 5, place(pair, ring + 4 - turn[t]))

    def second_relay(t):
        owner = place(pair, ring + 2)
        got(t, owner)
        pass_on(t, owner, 6, place(1 - pair, ring))

    gather_student(0)
    gather_student(1)
    slope(0)
    gather_student(2)
    slope(1)
    first_relay(0)
    slope(2)
    first_relay(1)
    second_relay(0)
    first_relay(2)
    second_relay(1)
    second_relay(2)

    for t in range(3):
        got(t, place(pair, ring + turn[t]))
        got(t, place(1 - pair, ring + 4 - turn[t]))
        got(t, place(1 - pair, ring + turn[t]))
        got(t, place(1 - pair, ring + 2))
        units = slice(t * HB, (t + 1) * HB)
        back = nn(heads[t][...], slo[BASE[t] : BASE[t] + WIDTHS[t], :])
        inner[units, :] = (back * before[units, :]).astype(BF16)

    def up(i, _):
        q = lax.rem(m // 2 + 1 + i, 4)
        rows = pl.ds(aligned(q * 128, 128), 128)
        part2[rows, :] = nn(flipped(inner[:, rows]), ai[...].reshape(3 * HB, D)).astype(BF16)
        for k in range(2):
            p = q * 2 + k

            @pl.when(p != m)
            def _send():
                mine = part2.at[pl.ds(aligned(p * BLK, BLK), BLK)]
                remote(mine, rs3.at[m], row_s.at[2, p], row_r.at[2, m], {"mp": p}).start()

        return _

    lax.fori_loop(0, 4, up, 0)

    def to_partner(which, send, received):
        def body(k, _):
            j = k * 2 + (1 - core)
            remote(send.at[j], received.at[k], cor_s.at[which, k], cor_r.at[which, k], {"dp": partner}).start()
            return _

        lax.fori_loop(0, 8, body, 0)

    def onward(which, send, received, mid, last):
        def body(i, _):
            k = lax.rem(half + i, 8)
            remote(send.at[k], received.at[k], cor_s.at[which, k], cor_r.at[which, k], {"dp": partner}).wait_recv()
            mid[k] = (send[k * 2 + core].astype(F32) + received[k].astype(F32)).astype(BF16)

            @pl.when(k != half)
            def _send():
                remote(mid.at[k], last.at[half], dp_s.at[which, k], dp_r.at[which, half], {"dp": k * 2 + core}).start()

            return _

        lax.fori_loop(1, 9, body, 0)

    def reduced(which, mid, last, out):
        out[...] = mid[half].astype(F32)

        def body(i, _):
            k = lax.rem(half + i, 8)
            remote(mid.at[k], last.at[k], dp_s.at[which, k], dp_r.at[which, k], {"dp": k * 2 + core}).wait_recv()
            out[...] += last[k].astype(F32)
            return _

        lax.fori_loop(1, 8, body, 0)

    def pieces(dst, j, value):
        for k in range(4):
            dst[j * 4 + k] = value[k * DB : (k + 1) * DB].astype(BF16)

    for t in range(3):
        def head_grad(i, _, t=t):
            n = (384, 384, 640)[t]
            at = aligned(i * n, 128)
            rows = pl.ds(aligned(BASE[t] + at, 128), n)
            hf32[pl.ds(at, n), :] = nt(slo[rows, :], lift[t * HB : (t + 1) * HB, :])
            return _

        lax.fori_loop(0, WIDTHS[t] // (384, 384, 640)[t], head_grad, 0)

        def head_piece(j, _, t=t):
            rows = pl.ds(aligned(j * PB[t], 8), PB[t])
            hsend[j, HOFF[t] : HOFF[t] + PB[t], :] = hf32[rows, :].astype(BF16)
            return _

        lax.fori_loop(0, DP, head_piece, 0)
    to_partner(0, hsend, hcore)

    def adaptor_grad(j, _):
        pieces(asend, j, nt(finalt[pl.ds(aligned(j * 4 * DB, 16), 4 * DB), :], inner[...]))
        return _

    lax.fori_loop(0, DP // 4, adaptor_grad, 0)
    to_partner(1, asend, acore)
    onward(0, hsend, hcore, hmid, hrecv)
    onward(1, asend, acore, amid, arecv)

    upstream = gathered(part2, 2, rs3)
    scaled = upstream * fg[...]
    hat = normal[...]
    through = inverse[:, 0:1] * (
        scaled
        - jnp.mean(scaled, axis=-1, keepdims=True)
        - hat * jnp.mean(scaled * hat, axis=-1, keepdims=True)
    )
    thr[own_rows, :] = through.astype(BF16)
    spread(thr, 3)
    arrived(thr, 3)

    flip_all(thr, finalt)

    def narrow_grad(j, _):
        pieces(nsend, j, nn(finalt[pl.ds(aligned(j * 4 * DB, 16), 4 * DB), :], active[...]))
        return _

    lax.fori_loop(0, DP // 4, narrow_grad, 0)
    to_partner(2, nsend, ncore)
    def backward(i, _):
        rows = pl.ds(aligned(i * 128, 128), 128)
        active[rows, :] = (nt(thr[rows, :], nw[...]) * wide[rows, :]).astype(BF16)
        return _

    lax.fori_loop(0, 4, backward, 0)
    onward(2, nsend, ncore, nmid, nrecv)

    def widen_grad(j, _):
        pieces(wsend, j, nn(firstt[pl.ds(aligned(j * 4 * DB, 16), 4 * DB), :], active[...]))
        return _

    lax.fori_loop(0, DP // 4, widen_grad, 0)
    to_partner(3, wsend, wcore)
    onward(3, wsend, wcore, wmid, wrecv)
    reduced(0, hmid, hrecv, hacc)
    out_d[...] = hacc[0:96, :].T
    out_g[...] = hacc[96:168, :]
    out_s[...] = hacc[176:256, :].T
    reduced(1, amid, arecv, aacc)
    for t in range(3):
        out_a[t] = aacc[:, t * HB : (t + 1) * HB]
    reduced(2, nmid, nrecv, out_n)
    reduced(3, wmid, wrecv, out_w)

    def sent_dp(i, _):
        j = lax.rem(d + i, DP)
        remote(tsend.at[images_of(j)], trecv.at[images_of(d)], tea_s.at[j], tea_r.at[d], {"dp": j}).wait_send()
        return _

    lax.fori_loop(1, DP, sent_dp, 0)

    def sent_mp(i, _):
        p = mate(i)
        where = {"mp": p}
        for which, (src, dst) in enumerate(((part, rs1), (final, rs1), (part2, rs3), (thr, rs3))):
            remote(src.at[own_rows], dst.at[m], row_s.at[which, p], row_r.at[which, m], where).wait_send()
        for t in range(3):
            rows = pl.ds(aligned(BASE[t] + p * CB[t], 16), CB[t])
            there = rs2.at[m, OFF[t] : OFF[t] + CB[t]]
            remote(sp.at[rows], there, stu_s.at[t, p], stu_r.at[t, m], where).wait_send()
            remote(stats.at[t], statr.at[t, m], sta_s.at[t, p], sta_r.at[t, m], where).wait_send()
        return _

    lax.fori_loop(1, MP, sent_mp, 0)
    for t in range(3):
        for k in range(7):
            slope_copy(t, m, k, place(pair, ring + 1)).wait_send()
    reductions = (
        (hsend, hcore, hmid, hrecv),
        (asend, acore, amid, arecv),
        (nsend, ncore, nmid, nrecv),
        (wsend, wcore, wmid, wrecv),
    )

    def sent_core(k, _):
        for which, (send, received, mid, last) in enumerate(reductions):
            remote(send.at[k], received.at[k], cor_s.at[which, k], cor_r.at[which, k], {"dp": partner}).wait_send()
        return _

    lax.fori_loop(0, 8, sent_core, 0)

    def sent_chip(i, _):
        k = lax.rem(half + i, 8)
        for which, (send, received, mid, last) in enumerate(reductions):
            remote(mid.at[k], last.at[half], dp_s.at[which, k], dp_r.at[which, half], {"dp": k * 2 + core}).wait_send()
        return _

    lax.fori_loop(1, 8, sent_chip, 0)


def local(
    tokens, norm_gain, widen_weight, narrow_weight, final_gain, adaptor_in,
    head_dino, head_siglip, head_sam, teacher_dino, teacher_siglip, teacher_sam,
    step_lags, owner_slot,
):
    vmem = pl.BlockSpec(memory_space=pltpu.VMEM)

    def reduction(rows, columns):
        return [
            pltpu.VMEM((DP, rows, columns), BF16),
            pltpu.VMEM((8, rows, columns), BF16),
            pltpu.VMEM((8, rows, columns), BF16),
            pltpu.VMEM((8, rows, columns), BF16),
        ]

    dma = pltpu.SemaphoreType.DMA
    arrays = (
        tokens, widen_weight, narrow_weight,
        teacher_dino.transpose(0, 2, 1), teacher_siglip.transpose(0, 2, 1), teacher_sam.transpose(0, 2, 1),
        adaptor_in.transpose(0, 2, 1), head_dino, head_siglip, head_sam,
    )
    w, n, a, dino, siglip, sam = pl.pallas_call(
        kernel,
        out_shape=(
            jax.ShapeDtypeStruct((DB, FB), F32),
            jax.ShapeDtypeStruct((DB, FB), F32),
            jax.ShapeDtypeStruct((3, DB, HB), F32),
            jax.ShapeDtypeStruct((HB, PB[0]), F32),
            jax.ShapeDtypeStruct((PB[1], HB), F32),
            jax.ShapeDtypeStruct((HB, PB[2]), F32),
        ),
        in_specs=[pl.BlockSpec(memory_space=pltpu.SMEM)] + [vmem] * 3 + [pl.BlockSpec(memory_space=pl.ANY)] * 10,
        out_specs=(vmem,) * 6,
        scratch_shapes=[
            *[pltpu.VMEM(array.shape, array.dtype) for array in arrays],
            dma((len(arrays),)),
            pltpu.VMEM((R, D), BF16),
            pltpu.VMEM((R, FB), F32),
            pltpu.VMEM((R, FB), BF16),
            pltpu.VMEM((R, D), BF16),
            pltpu.VMEM((MP, BLK, D), BF16),
            pltpu.VMEM((R, D), BF16),
            pltpu.VMEM((BLK, D), F32),
            pltpu.VMEM((BLK, 128), F32),
            pltpu.VMEM((CH, HB), BF16),
            pltpu.VMEM((3 * HB, R), F32),
            pltpu.VMEM((3 * HB, R), BF16),
            pltpu.VMEM((CH, R), BF16),
            pltpu.VMEM((MP, CBS, R), BF16),
            pltpu.VMEM((CBS, R), F32),
            pltpu.VMEM((R, 768), BF16),
            pltpu.VMEM((R, 768), BF16),
            pltpu.VMEM((CBS, R), BF16),
            pltpu.VMEM((3, 8, R), F32),
            pltpu.VMEM((3, MP, 8, R), F32),
            pltpu.VMEM((CH, R), BF16),
            pltpu.VMEM((3 * HB, R), BF16),
            pltpu.VMEM((R, D), BF16),
            pltpu.VMEM((MP, BLK, D), BF16),
            pltpu.VMEM((R, D), BF16),
            pltpu.VMEM((D, R), BF16),
            pltpu.VMEM((D, R), BF16),
            pltpu.VMEM((1536, HB), F32),
            pltpu.VMEM((256, HB), F32),
            pltpu.VMEM((DB, 3 * HB), F32),
            *reduction(256, HB),
            *reduction(DB, 3 * HB),
            *reduction(DB, FB),
            *reduction(DB, FB),
            dma((4, MP)), dma((4, MP)),
            dma((DP,)), dma((DP,)),
            dma((3, MP)), dma((3, MP)),
            dma((3, MP)), dma((3, MP)),
            dma((3, MP)), dma((3, MP)),
            dma((4, 8)), dma((4, 8)),
            dma((4, 8)), dma((4, 8)),
        ],
        compiler_params=pltpu.CompilerParams(
            collective_id=0, has_side_effects=True, vmem_limit_bytes=66_000_000
        ),
        name="step",
    )(
        step_lags, owner_slot[None], norm_gain[None], final_gain[None], *arrays
    )
    return w.T, n.T, a, dino, siglip.T, sam


def solution(mesh):
    placed = (
        P("dp", None),
        P(),
        P(None, "mp"),
        P("mp", None),
        P(),
        P(None, None, "mp"),
        P("mp", None),
        P("mp", None),
        P("mp", None),
        P(None, "dp", "mp"),
        P(None, "dp", "mp"),
        P(None, "dp", "mp"),
        P(),
        P(),
    )
    return jax.shard_map(
        local,
        mesh=mesh,
        in_specs=placed,
        out_specs=(
            P("mp", "dp"),
            P("mp", "dp"),
            P(None, "dp", "mp"),
            P("mp", "dp"),
            P("mp", "dp"),
            P("mp", "dp"),
        ),
        check_vma=False,
    )
```

```python
import jax
import jax.numpy as jnp
from jax import lax
from jax.experimental import pallas as pl
from jax.experimental.pallas import tpu as pltpu
from jax.sharding import PartitionSpec as P

F32, BF16 = jnp.float32, jnp.bfloat16
MESH = pl.DeviceIdType.MESH

R, D, FB, HB = 512, 1280, 640, 160
DP, MP, PATCH = 16, 8, 32
WIDTHS = (1536, 1152, 1280)
CB = tuple(w // MP for w in WIDTHS)
PB = tuple(w // DP for w in WIDTHS)
BASE = (0, 1536, 2688)
OFF = (0, 192, 336)
HOFF = (0, 96, 176)
CH, CBS = 3968, 496
BLK = R // MP
DB = D // DP

slope_coef = 0.7978845608028654
cubic_coef = 0.044715


def smooth(value):
    return 0.5 * value * (1.0 + jnp.tanh(slope_coef * (value + cubic_coef * value * value * value)))


def smooth_slope(value):
    square = value * value
    tangent = jnp.tanh(slope_coef * (value + cubic_coef * value * square))
    return 0.5 * (1.0 + tangent) + 0.5 * value * (1.0 - tangent * tangent) * slope_coef * (
        1.0 + 3.0 * cubic_coef * square
    )


def nn(a, b):
    return lax.dot_general(a, b, (((1,), (0,)), ((), ())), preferred_element_type=F32)


def nt(a, b):
    return lax.dot_general(a, b, (((1,), (1,)), ((), ())), preferred_element_type=F32)


def eye(n):
    return (
        lax.broadcasted_iota(jnp.int32, (n, n), 0) == lax.broadcasted_iota(jnp.int32, (n, n), 1)
    ).astype(F32).astype(BF16)


def flipped(block):
    return nt(eye(block.shape[1]), block).astype(BF16)


def remote(src, dst, send, recv, where):
    return pltpu.make_async_remote_copy(
        src_ref=src, dst_ref=dst, send_sem=send, recv_sem=recv, device_id=where, device_id_type=MESH
    )


def aligned(value, n):
    return pl.multiple_of(value, n)


def kernel(
    lags, slots, ng, fg, *refs,
):
    outside, refs = refs[:10], refs[10:]
    outputs, inside, load_sem, refs = refs[:6], refs[6:16], refs[16], refs[17:]
    step(lags, slots, ng, fg, outside, load_sem, *inside, *outputs, *refs)


def step(
    lags, slots, ng, fg, outside, load_sem, tok, ww, nw, t0, t1, t2, ai, h0, h1, h2,
    out_w, out_n, out_a, out_d, out_g, out_s,
    first, wide, active, part, rs1, final, normal, inverse,
    headt, before, lift, sp, rs2, stu, tsend, trecv, tgt, stats, statr,
    slo, inner, part2, rs3, thr, finalt, firstt,
    hf32, hacc, aacc, hsend, hcore, hmid, hrecv, asend, acore, amid, arecv,
    nsend, ncore, nmid, nrecv, wsend, wcore, wmid, wrecv,
    row_s, row_r, tea_s, tea_r, stu_s, stu_r, sta_s, sta_r, slo_s, slo_r,
    cor_s, cor_r, dp_s, dp_r,
):
    d = lax.axis_index("dp")
    m = lax.axis_index("mp")
    core = lax.rem(d, 2)
    half = d // 2
    loads = [
        pltpu.make_async_copy(src, dst, load_sem.at[k])
        for k, (src, dst) in enumerate(zip(outside, (tok, ww, nw, t0, t1, t2, ai, h0, h1, h2)))
    ]
    heads = (h0, h1, h2)
    teachers = (t0, t1, t2)
    partner = half * 2 + (1 - core)

    def mate(i):
        return lax.rem(m + i, MP)

    def greet(i, _):
        pl.semaphore_signal(barrier, inc=1, device_id={"mp": mate(i)}, device_id_type=MESH)
        return _

    def greet_dp(i, _):
        pl.semaphore_signal(barrier, inc=1, device_id={"dp": lax.rem(d + i, DP)}, device_id_type=MESH)
        return _

    barrier = pltpu.get_barrier_semaphore()
    lax.fori_loop(1, MP, greet, 0)
    lax.fori_loop(1, DP, greet_dp, 0)
    for load in loads:
        load.start()
    loads[0].wait()

    def normalized(i, _):
        rows = pl.ds(aligned(i * 128, 128), 128)
        value = tok[rows, :].astype(F32)
        centre = value - jnp.mean(value, axis=-1, keepdims=True)
        inv = lax.rsqrt(jnp.mean(centre * centre, axis=-1, keepdims=True) + 1e-06)
        first[rows, :] = (centre * inv * ng[...]).astype(BF16)
        return _

    lax.fori_loop(0, 4, normalized, 0)
    loads[1].wait()
    loads[2].wait()
    pl.semaphore_wait(barrier, MP - 1 + DP - 1)

    def forward(i, _):
        q = lax.rem(m // 2 + 1 + i, 4)
        rows = pl.ds(aligned(q * 128, 128), 128)
        w = nn(first[rows, :], ww[...])
        wide[rows, :] = w
        active[rows, :] = smooth(w).astype(BF16)
        part[rows, :] = nn(active[rows, :], nw[...]).astype(BF16)
        for k in range(2):
            p = q * 2 + k

            @pl.when(p != m)
            def _send():
                mine = part.at[pl.ds(aligned(p * BLK, BLK), BLK)]
                remote(mine, rs1.at[m], row_s.at[0, p], row_r.at[0, m], {"mp": p}).start()

        return _

    lax.fori_loop(0, 4, forward, 0)

    def slopes_of(ref, n):
        def body(i, _):
            rows = pl.ds(aligned(i * 32, 32), 32)
            ref[rows, :] = smooth_slope(ref[rows, :])
            return _

        lax.fori_loop(0, n // 32, body, 0)

    def grid(shape, dim):
        return lax.broadcasted_iota(jnp.int32, shape, dim)

    def ones_where(condition):
        return condition.astype(F32).astype(BF16)

    for load in loads[3:]:
        load.wait()
    slot = slots[...].reshape(1, DP * DP)
    spread_out = ones_where(grid((DP * DP, R), 0) == d * DP + grid((DP * DP, R), 1) // PATCH)
    own_slot = nn(jnp.broadcast_to(slot, (16, DP * DP)).astype(F32).astype(BF16), spread_out)[0:1]
    goes = own_slot.astype(jnp.int32) // DP
    same_patch = lax.rem(grid((R, R), 0), PATCH) == lax.rem(grid((R, R), 1), PATCH)
    chosen = ones_where((goes == grid((R, R), 0) // PATCH) & same_patch)
    for t in range(3):
        late = (lags[t] - 1).astype(F32)
        stale = teachers[t][0].astype(F32) * (1.0 - late) + teachers[t][1].astype(F32) * late
        tsend[:, 256 * t : 256 * t + CB[t]] = nt(chosen, stale.astype(BF16)).astype(BF16)

    def images_of(j):
        return pl.ds(aligned(j * PATCH, PATCH), PATCH)

    def teach(i, _):
        j = lax.rem(d + i, DP)
        remote(tsend.at[images_of(j)], trecv.at[images_of(d)], tea_s.at[j], tea_r.at[d], {"dp": j}).start()
        return _

    lax.fori_loop(1, DP, teach, 0)
    trecv[images_of(d), :] = tsend[images_of(d), :]

    slopes_of(wide, R)
    for t in range(3):
        def head_block(i, _, t=t):
            at = aligned(i * 128, 128)
            headt[pl.ds(aligned(BASE[t] + at, 128), 128), :] = flipped(heads[t][:, pl.ds(at, 128)])
            return _

        lax.fori_loop(0, WIDTHS[t] // 128, head_block, 0)

    own_rows = pl.ds(aligned(m * BLK, BLK), BLK)

    def gathered(buffer, which, received):
        total = buffer[own_rows, :].astype(F32)
        for i in range(1, MP):
            p = mate(i)
            remote(received.at[p], received.at[p], row_s.at[which, p], row_r.at[which, p], {"mp": p}).wait_recv()
            total = total + received[p].astype(F32)
        return total

    def spread(buffer, which):
        def body(i, _):
            p = mate(i)
            remote(buffer.at[own_rows], buffer.at[own_rows], row_s.at[which, p], row_r.at[which, m], {"mp": p}).start()
            return _

        lax.fori_loop(1, MP, body, 0)

    def arrived(buffer, which):
        def body(i, _):
            p = mate(i)
            there = buffer.at[pl.ds(aligned(p * BLK, BLK), BLK)]
            remote(there, there, row_s.at[which, p], row_r.at[which, p], {"mp": p}).wait_recv()
            return _

        lax.fori_loop(1, MP, body, 0)

    hidden = tok[own_rows, :].astype(F32) + gathered(part, 0, rs1)
    centre = hidden - jnp.mean(hidden, axis=-1, keepdims=True)
    inv = lax.rsqrt(jnp.mean(centre * centre, axis=-1, keepdims=True) + 1e-06)
    normal[...] = centre * inv
    inverse[...] = jnp.broadcast_to(inv, (BLK, 128))
    final[own_rows, :] = (normal[...] * fg[...]).astype(BF16)
    spread(final, 1)

    def landed(i, _):
        j = lax.rem(d + i, DP)
        remote(tsend.at[images_of(j)], trecv.at[images_of(j)], tea_s.at[j], tea_r.at[j], {"dp": j}).wait_recv()
        return _

    lax.fori_loop(1, DP, landed, 0)

    holds = ones_where(slot == d * DP + grid((R, DP * DP), 0) // PATCH)
    group = ones_where(grid((R, DP * DP), 1) // DP == grid((R, DP * DP), 0) // PATCH)
    placing = jnp.where(same_patch, nt(group, holds), 0.0).astype(BF16)
    for t in range(3):
        block = flipped(trecv[:, 256 * t : 256 * t + CB[t]])
        tgt[OFF[t] : OFF[t] + CB[t], :] = nn(block, placing).astype(BF16)

    arrived(final, 1)

    pair, ring = m // 4, lax.rem(m, 4)

    def place(a, b):
        return a * 4 + lax.rem(b, 4)

    def channels(t, p):
        return pl.ds(aligned(BASE[t] + p * CB[t], 16), CB[t])

    def stu_copy(t, p, slot, k, to):
        there = rs2.at[slot, OFF[t] : OFF[t] + CB[t]]
        return remote(sp.at[channels(t, p)], there, stu_s.at[t, k], stu_r.at[t, slot], {"mp": to})

    def stu_got(t, slot):
        stu_copy(t, m, slot, slot, place(1 - pair, ring)).wait_recv()
        return rs2[slot, OFF[t] : OFF[t] + CB[t]].astype(F32)

    for t in range(3):
        units = slice(t * HB, (t + 1) * HB)
        b = nt(ai[t], final[...])
        before[units, :] = b
        lift[units, :] = smooth(b).astype(BF16)

        def student(p, t=t, units=units):
            rows = channels(t, p)
            sp[rows, :] = nn(headt[rows, :], lift[units, :]).astype(BF16)

        if t == 0:
            def over_pair(i, _, student=student):
                y = lax.rem(ring + i, 4)
                student(place(1 - pair, y))
                stu_copy(0, place(1 - pair, y), y, y, place(1 - pair, ring)).start()
                return _

            def kept(i, _, student=student):
                student(place(pair, ring + i))
                return _

            lax.fori_loop(0, 4, over_pair, 0)
            lax.fori_loop(0, 4, kept, 0)
        else:
            def over_ring(i, _, t=t, student=student):
                y, c = lax.rem(ring + 1 + i // 2, 4), lax.rem(i, 2)
                student(place(c, y))
                stu_copy(t, place(c, y), ring * 2 + c, y * 2 + c, place(pair, y)).start()
                return _

            def kept(i, _, student=student):
                student(place(i, ring))
                return _

            lax.fori_loop(0, 6, over_ring, 0)
            lax.fori_loop(0, 2, kept, 0)

    slopes_of(before, 3 * HB)

    def flip_all(src, dst):
        def body(i, _):
            at = aligned(i * 128, 128)
            dst[pl.ds(at, 128), :] = flipped(src[:, pl.ds(at, 128)])
            return _

        lax.fori_loop(0, D // 128, body, 0)

    flip_all(final, finalt)
    flip_all(first, firstt)

    def half_summed(t):
        mine = slice(OFF[t], OFF[t] + CB[t])
        if t == 0:
            def body(i, _):
                y = lax.rem(ring + i, 4)
                rows = channels(0, place(pair, y))
                sp[rows, :] = (sp[rows, :].astype(F32) + stu_got(0, y)).astype(BF16)
                stu_copy(0, place(pair, y), 4 + ring, 4 + y, place(pair, y)).start()
                return _

            lax.fori_loop(1, 4, body, 0)
            stu[mine, :] = sp[channels(0, m), :].astype(F32) + stu_got(0, ring)
        else:
            other = channels(t, place(1 - pair, ring))
            total = sp[other, :].astype(F32)
            for i in range(1, 4):
                total = total + stu_got(t, lax.rem(ring + i, 4) * 2 + 1 - pair)
            sp[other, :] = total.astype(BF16)
            stu_copy(t, place(1 - pair, ring), ring * 2, ring * 2, place(1 - pair, ring)).start()
            total = sp[channels(t, m), :].astype(F32)
            for i in range(1, 4):
                total = total + stu_got(t, lax.rem(ring + i, 4) * 2 + pair)
            stu[mine, :] = total

    def gather_student(t):
        mine = slice(OFF[t], OFF[t] + CB[t])
        if t == 0:
            for i in range(1, 4):
                stu[mine, :] += stu_got(0, 4 + lax.rem(ring + i, 4))
        else:
            stu[mine, :] += stu_got(t, ring * 2)
        y = stu[mine, :]
        f = tgt[mine, :].astype(F32)
        stats[t, 0:1, :] = jnp.sum(y * f, axis=0, keepdims=True)
        stats[t, 1:2, :] = jnp.sum(y * y, axis=0, keepdims=True)
        stats[t, 2:3, :] = jnp.sum(f * f, axis=0, keepdims=True)
        stats[t, 3:8, :] = jnp.zeros((5, R), F32)

        def send(i, _):
            p = mate(i)
            remote(stats.at[t], statr.at[t, m], sta_s.at[t, p], sta_r.at[t, m], {"mp": p}).start()
            return _

        lax.fori_loop(1, MP, send, 0)

    def slope(t):
        mine = slice(OFF[t], OFF[t] + CB[t])
        total = stats[t]
        for i in range(1, MP):
            p = mate(i)
            remote(stats.at[t], statr.at[t, p], sta_s.at[t, p], sta_r.at[t, p], {"mp": p}).wait_recv()
            total = total + statr[t, p]
        square_student = total[1:2] + 1e-06
        joint = lax.rsqrt(square_student * (total[2:3] + 1e-06))
        scale = total[0:1] * joint / square_student
        rows = pl.ds(aligned(BASE[t] + m * CB[t], 16), CB[t])
        slo[rows, :] = (scale * stu[mine, :] - joint * tgt[mine, :].astype(F32)).astype(BF16)

        pass_on(t, m, 0, place(pair, ring + 1))
        pass_on(t, m, 1, place(pair, ring + 3))
        pass_on(t, m, 2, place(1 - pair, ring))

    turn = (1, 3, 3)

    def slope_copy(t, owner, k, to):
        block = slo.at[pl.ds(aligned(BASE[t] + owner * CB[t], 16), CB[t])]
        return remote(block, block, slo_s.at[t, k], slo_r.at[t, owner], {"mp": to})

    def pass_on(t, owner, k, to):
        slope_copy(t, owner, k, to).start()

    def got(t, owner):
        slope_copy(t, owner, 0, owner).wait_recv()

    def first_relay(t):
        owner = place(pair, ring + 4 - turn[t])
        got(t, owner)
        pass_on(t, owner, 3, place(pair, ring + turn[t]))
        owner = place(1 - pair, ring)
        got(t, owner)
        pass_on(t, owner, 4, place(pair, ring + turn[t]))
        pass_on(t, owner, 5, place(pair, ring + 4 - turn[t]))

    def second_relay(t):
        owner = place(pair, ring + 2)
        got(t, owner)
        pass_on(t, owner, 6, place(1 - pair, ring))

    half_summed(1)
    half_summed(0)
    gather_student(1)
    half_summed(2)
    slope(1)
    gather_student(0)
    gather_student(2)
    first_relay(1)
    slope(0)
    slope(2)
    first_relay(0)
    second_relay(1)
    first_relay(2)
    second_relay(0)
    second_relay(2)

    for t in (1, 0, 2):
        got(t, place(pair, ring + turn[t]))
        got(t, place(1 - pair, ring + 4 - turn[t]))
        got(t, place(1 - pair, ring + turn[t]))
        got(t, place(1 - pair, ring + 2))
        units = slice(t * HB, (t + 1) * HB)
        back = nn(heads[t][...], slo[BASE[t] : BASE[t] + WIDTHS[t], :])
        inner[units, :] = (back * before[units, :]).astype(BF16)

    def up(i, _):
        q = lax.rem(m // 2 + 1 + i, 4)
        rows = pl.ds(aligned(q * 128, 128), 128)
        part2[rows, :] = nn(flipped(inner[:, rows]), ai[...].reshape(3 * HB, D)).astype(BF16)
        for k in range(2):
            p = q * 2 + k

            @pl.when(p != m)
            def _send():
                mine = part2.at[pl.ds(aligned(p * BLK, BLK), BLK)]
                remote(mine, rs3.at[m], row_s.at[2, p], row_r.at[2, m], {"mp": p}).start()

        return _

    lax.fori_loop(0, 4, up, 0)

    def to_partner(which, send, received):
        def body(k, _):
            j = k * 2 + (1 - core)
            remote(send.at[j], received.at[k], cor_s.at[which, k], cor_r.at[which, k], {"dp": partner}).start()
            return _

        lax.fori_loop(0, 8, body, 0)

    def onward(which, send, received, mid, last):
        def body(i, _):
            k = lax.rem(half + i, 8)
            remote(send.at[k], received.at[k], cor_s.at[which, k], cor_r.at[which, k], {"dp": partner}).wait_recv()
            mid[k] = (send[k * 2 + core].astype(F32) + received[k].astype(F32)).astype(BF16)

            @pl.when(k != half)
            def _send():
                remote(mid.at[k], last.at[half], dp_s.at[which, k], dp_r.at[which, half], {"dp": k * 2 + core}).start()

            return _

        lax.fori_loop(1, 9, body, 0)

    def reduced(which, mid, last, out):
        out[...] = mid[half].astype(F32)

        def body(i, _):
            k = lax.rem(half + i, 8)
            remote(mid.at[k], last.at[k], dp_s.at[which, k], dp_r.at[which, k], {"dp": k * 2 + core}).wait_recv()
            out[...] += last[k].astype(F32)
            return _

        lax.fori_loop(1, 8, body, 0)

    def pieces(dst, j, value):
        for k in range(4):
            dst[j * 4 + k] = value[k * DB : (k + 1) * DB].astype(BF16)

    for t in range(3):
        def head_grad(i, _, t=t):
            n = (384, 384, 640)[t]
            at = aligned(i * n, 128)
            rows = pl.ds(aligned(BASE[t] + at, 128), n)
            hf32[pl.ds(at, n), :] = nt(slo[rows, :], lift[t * HB : (t + 1) * HB, :])
            return _

        lax.fori_loop(0, WIDTHS[t] // (384, 384, 640)[t], head_grad, 0)

        def head_piece(j, _, t=t):
            rows = pl.ds(aligned(j * PB[t], 8), PB[t])
            hsend[j, HOFF[t] : HOFF[t] + PB[t], :] = hf32[rows, :].astype(BF16)
            return _

        lax.fori_loop(0, DP, head_piece, 0)
    to_partner(0, hsend, hcore)

    def adaptor_grad(j, _):
        pieces(asend, j, nt(finalt[pl.ds(aligned(j * 4 * DB, 16), 4 * DB), :], inner[...]))
        return _

    lax.fori_loop(0, DP // 4, adaptor_grad, 0)
    to_partner(1, asend, acore)
    onward(0, hsend, hcore, hmid, hrecv)
    onward(1, asend, acore, amid, arecv)

    upstream = gathered(part2, 2, rs3)
    scaled = upstream * fg[...]
    hat = normal[...]
    through = inverse[:, 0:1] * (
        scaled
        - jnp.mean(scaled, axis=-1, keepdims=True)
        - hat * jnp.mean(scaled * hat, axis=-1, keepdims=True)
    )
    thr[own_rows, :] = through.astype(BF16)
    spread(thr, 3)
    arrived(thr, 3)

    flip_all(thr, finalt)

    def narrow_grad(j, _):
        pieces(nsend, j, nn(finalt[pl.ds(aligned(j * 4 * DB, 16), 4 * DB), :], active[...]))
        return _

    lax.fori_loop(0, DP // 4, narrow_grad, 0)
    to_partner(2, nsend, ncore)
    def backward(i, _):
        rows = pl.ds(aligned(i * 128, 128), 128)
        active[rows, :] = (nt(thr[rows, :], nw[...]) * wide[rows, :]).astype(BF16)
        return _

    lax.fori_loop(0, 4, backward, 0)
    onward(2, nsend, ncore, nmid, nrecv)

    def widen_grad(j, _):
        pieces(wsend, j, nn(firstt[pl.ds(aligned(j * 4 * DB, 16), 4 * DB), :], active[...]))
        return _

    lax.fori_loop(0, DP // 4, widen_grad, 0)
    to_partner(3, wsend, wcore)
    onward(3, wsend, wcore, wmid, wrecv)
    reduced(0, hmid, hrecv, hacc)
    out_d[...] = hacc[0:96, :].T
    out_g[...] = hacc[96:168, :]
    out_s[...] = hacc[176:256, :].T
    reduced(1, amid, arecv, aacc)
    for t in range(3):
        out_a[t] = aacc[:, t * HB : (t + 1) * HB]
    reduced(2, nmid, nrecv, out_n)
    reduced(3, wmid, wrecv, out_w)

    def sent_dp(i, _):
        j = lax.rem(d + i, DP)
        remote(tsend.at[images_of(j)], trecv.at[images_of(d)], tea_s.at[j], tea_r.at[d], {"dp": j}).wait_send()
        return _

    lax.fori_loop(1, DP, sent_dp, 0)

    def sent_mp(i, _):
        p = mate(i)
        where = {"mp": p}
        for which, (src, dst) in enumerate(((part, rs1), (final, rs1), (part2, rs3), (thr, rs3))):
            remote(src.at[own_rows], dst.at[m], row_s.at[which, p], row_r.at[which, m], where).wait_send()
        for t in range(3):
            remote(stats.at[t], statr.at[t, m], sta_s.at[t, p], sta_r.at[t, m], where).wait_send()
        return _

    lax.fori_loop(1, MP, sent_mp, 0)
    for t in range(3):
        for k in range(7):
            slope_copy(t, m, k, place(pair, ring + 1)).wait_send()
        for i in range(1, 4):
            y = lax.rem(ring + i, 4)
            if t == 0:
                stu_copy(0, m, y, y, place(1 - pair, ring)).wait_send()
                stu_copy(0, m, y, 4 + y, place(1 - pair, ring)).wait_send()
            else:
                stu_copy(t, m, y, y * 2, place(1 - pair, ring)).wait_send()
                stu_copy(t, m, y, y * 2 + 1, place(1 - pair, ring)).wait_send()
        k = ring if t == 0 else ring * 2
        stu_copy(t, m, k, k, place(1 - pair, ring)).wait_send()
    reductions = (
        (hsend, hcore, hmid, hrecv),
        (asend, acore, amid, arecv),
        (nsend, ncore, nmid, nrecv),
        (wsend, wcore, wmid, wrecv),
    )

    def sent_core(k, _):
        for which, (send, received, mid, last) in enumerate(reductions):
            remote(send.at[k], received.at[k], cor_s.at[which, k], cor_r.at[which, k], {"dp": partner}).wait_send()
        return _

    lax.fori_loop(0, 8, sent_core, 0)

    def sent_chip(i, _):
        k = lax.rem(half + i, 8)
        for which, (send, received, mid, last) in enumerate(reductions):
            remote(mid.at[k], last.at[half], dp_s.at[which, k], dp_r.at[which, half], {"dp": k * 2 + core}).wait_send()
        return _

    lax.fori_loop(1, 8, sent_chip, 0)


def local(
    tokens, norm_gain, widen_weight, narrow_weight, final_gain, adaptor_in,
    head_dino, head_siglip, head_sam, teacher_dino, teacher_siglip, teacher_sam,
    step_lags, owner_slot,
):
    vmem = pl.BlockSpec(memory_space=pltpu.VMEM)

    def reduction(rows, columns):
        return [
            pltpu.VMEM((DP, rows, columns), BF16),
            pltpu.VMEM((8, rows, columns), BF16),
            pltpu.VMEM((8, rows, columns), BF16),
            pltpu.VMEM((8, rows, columns), BF16),
        ]

    dma = pltpu.SemaphoreType.DMA
    arrays = (
        tokens, widen_weight, narrow_weight,
        teacher_dino.transpose(0, 2, 1), teacher_siglip.transpose(0, 2, 1), teacher_sam.transpose(0, 2, 1),
        adaptor_in.transpose(0, 2, 1), head_dino, head_siglip, head_sam,
    )
    w, n, a, dino, siglip, sam = pl.pallas_call(
        kernel,
        out_shape=(
            jax.ShapeDtypeStruct((DB, FB), F32),
            jax.ShapeDtypeStruct((DB, FB), F32),
            jax.ShapeDtypeStruct((3, DB, HB), F32),
            jax.ShapeDtypeStruct((HB, PB[0]), F32),
            jax.ShapeDtypeStruct((PB[1], HB), F32),
            jax.ShapeDtypeStruct((HB, PB[2]), F32),
        ),
        in_specs=[pl.BlockSpec(memory_space=pltpu.SMEM)] + [vmem] * 3 + [pl.BlockSpec(memory_space=pl.ANY)] * 10,
        out_specs=(vmem,) * 6,
        scratch_shapes=[
            *[pltpu.VMEM(array.shape, array.dtype) for array in arrays],
            dma((len(arrays),)),
            pltpu.VMEM((R, D), BF16),
            pltpu.VMEM((R, FB), F32),
            pltpu.VMEM((R, FB), BF16),
            pltpu.VMEM((R, D), BF16),
            pltpu.VMEM((MP, BLK, D), BF16),
            pltpu.VMEM((R, D), BF16),
            pltpu.VMEM((BLK, D), F32),
            pltpu.VMEM((BLK, 128), F32),
            pltpu.VMEM((CH, HB), BF16),
            pltpu.VMEM((3 * HB, R), F32),
            pltpu.VMEM((3 * HB, R), BF16),
            pltpu.VMEM((CH, R), BF16),
            pltpu.VMEM((MP, CBS, R), BF16),
            pltpu.VMEM((CBS, R), F32),
            pltpu.VMEM((R, 768), BF16),
            pltpu.VMEM((R, 768), BF16),
            pltpu.VMEM((CBS, R), BF16),
            pltpu.VMEM((3, 8, R), F32),
            pltpu.VMEM((3, MP, 8, R), F32),
            pltpu.VMEM((CH, R), BF16),
            pltpu.VMEM((3 * HB, R), BF16),
            pltpu.VMEM((R, D), BF16),
            pltpu.VMEM((MP, BLK, D), BF16),
            pltpu.VMEM((R, D), BF16),
            pltpu.VMEM((D, R), BF16),
            pltpu.VMEM((D, R), BF16),
            pltpu.VMEM((1536, HB), F32),
            pltpu.VMEM((256, HB), F32),
            pltpu.VMEM((DB, 3 * HB), F32),
            *reduction(256, HB),
            *reduction(DB, 3 * HB),
            *reduction(DB, FB),
            *reduction(DB, FB),
            dma((4, MP)), dma((4, MP)),
            dma((DP,)), dma((DP,)),
            dma((3, MP)), dma((3, MP)),
            dma((3, MP)), dma((3, MP)),
            dma((3, MP)), dma((3, MP)),
            dma((4, 8)), dma((4, 8)),
            dma((4, 8)), dma((4, 8)),
        ],
        compiler_params=pltpu.CompilerParams(
            collective_id=0, has_side_effects=True, vmem_limit_bytes=66_000_000
        ),
        name="step",
    )(
        step_lags, owner_slot[None], norm_gain[None], final_gain[None], *arrays
    )
    return w.T, n.T, a, dino, siglip.T, sam


def solution(mesh):
    placed = (
        P("dp", None),
        P(),
        P(None, "mp"),
        P("mp", None),
        P(),
        P(None, None, "mp"),
        P("mp", None),
        P("mp", None),
        P("mp", None),
        P(None, "dp", "mp"),
        P(None, "dp", "mp"),
        P(None, "dp", "mp"),
        P(),
        P(),
    )
    return jax.shard_map(
        local,
        mesh=mesh,
        in_specs=placed,
        out_specs=(
            P("mp", "dp"),
            P("mp", "dp"),
            P(None, "dp", "mp"),
            P("mp", "dp"),
            P("mp", "dp"),
            P("mp", "dp"),
        ),
        check_vma=False,
    )
```

```python
import jax
import jax.numpy as jnp
from jax import lax
from jax.experimental import pallas as pl
from jax.experimental.pallas import tpu as pltpu
from jax.sharding import PartitionSpec as P

F32, BF16 = jnp.float32, jnp.bfloat16
MESH = pl.DeviceIdType.MESH

R, D, FB, HB = 512, 1280, 640, 160
DP, MP, PATCH = 16, 8, 32
WIDTHS = (1536, 1152, 1280)
CB = tuple(w // MP for w in WIDTHS)
PB = tuple(w // DP for w in WIDTHS)
BASE = (0, 1536, 2688)
OFF = (0, 192, 336)
HOFF = (0, 96, 176)
CH, CBS = 3968, 496
BLK = R // MP
DB = D // DP

slope_coef = 0.7978845608028654
cubic_coef = 0.044715


def smooth(value):
    return 0.5 * value * (1.0 + jnp.tanh(slope_coef * (value + cubic_coef * value * value * value)))


def smooth_slope(value):
    square = value * value
    tangent = jnp.tanh(slope_coef * (value + cubic_coef * value * square))
    return 0.5 * (1.0 + tangent) + 0.5 * value * (1.0 - tangent * tangent) * slope_coef * (
        1.0 + 3.0 * cubic_coef * square
    )


def nn(a, b):
    return lax.dot_general(a, b, (((1,), (0,)), ((), ())), preferred_element_type=F32)


def nt(a, b):
    return lax.dot_general(a, b, (((1,), (1,)), ((), ())), preferred_element_type=F32)


def eye(n):
    return (
        lax.broadcasted_iota(jnp.int32, (n, n), 0) == lax.broadcasted_iota(jnp.int32, (n, n), 1)
    ).astype(F32).astype(BF16)


def flipped(block):
    return nt(eye(block.shape[1]), block).astype(BF16)


def remote(src, dst, send, recv, where):
    return pltpu.make_async_remote_copy(
        src_ref=src, dst_ref=dst, send_sem=send, recv_sem=recv, device_id=where, device_id_type=MESH
    )


def aligned(value, n):
    return pl.multiple_of(value, n)


def kernel(
    lags, slots, ng, fg, *refs,
):
    outside, refs = refs[:10], refs[10:]
    outputs, inside, load_sem, refs = refs[:6], refs[6:16], refs[16], refs[17:]
    step(lags, slots, ng, fg, outside, load_sem, *inside, *outputs, *refs)


def step(
    lags, slots, ng, fg, outside, load_sem, tok, ww, nw, t0, t1, t2, ai, h0, h1, h2,
    out_w, out_n, out_a, out_d, out_g, out_s,
    first, wide, active, part, rs1, final, normal, inverse,
    headt, before, lift, sp, rs2, stu, tsend, trecv, tgt, stats, statr,
    slo, inner, part2, rs3, thr, finalt, firstt,
    hf32, hacc, aacc, hsend, hcore, hmid, hrecv, asend, acore, amid, arecv,
    nsend, ncore, nmid, nrecv, wsend, wcore, wmid, wrecv,
    row_s, row_r, tea_s, tea_r, stu_s, stu_r, sta_s, sta_r, slo_s, slo_r,
    cor_s, cor_r, dp_s, dp_r,
):
    d = lax.axis_index("dp")
    m = lax.axis_index("mp")
    core = lax.rem(d, 2)
    half = d // 2
    loads = [
        pltpu.make_async_copy(src, dst, load_sem.at[k])
        for k, (src, dst) in enumerate(zip(outside, (tok, ww, nw, t0, t1, t2, ai, h0, h1, h2)))
    ]
    heads = (h0, h1, h2)
    teachers = (t0, t1, t2)
    partner = half * 2 + (1 - core)

    def mate(i):
        return lax.rem(m + i, MP)

    def greet(i, _):
        pl.semaphore_signal(barrier, inc=1, device_id={"mp": mate(i)}, device_id_type=MESH)
        return _

    def greet_dp(i, _):
        pl.semaphore_signal(barrier, inc=1, device_id={"dp": lax.rem(d + i, DP)}, device_id_type=MESH)
        return _

    barrier = pltpu.get_barrier_semaphore()
    lax.fori_loop(1, MP, greet, 0)
    lax.fori_loop(1, DP, greet_dp, 0)
    for load in loads:
        load.start()
    loads[0].wait()

    def normalized(i, _):
        rows = pl.ds(aligned(i * 128, 128), 128)
        value = tok[rows, :].astype(F32)
        centre = value - jnp.mean(value, axis=-1, keepdims=True)
        inv = lax.rsqrt(jnp.mean(centre * centre, axis=-1, keepdims=True) + 1e-06)
        first[rows, :] = (centre * inv * ng[...]).astype(BF16)
        return _

    lax.fori_loop(0, 4, normalized, 0)
    loads[1].wait()
    loads[2].wait()
    pl.semaphore_wait(barrier, MP - 1 + DP - 1)

    def forward(i, _):
        q = lax.rem(m // 2 + 1 + i, 4)
        rows = pl.ds(aligned(q * 128, 128), 128)
        w = nn(first[rows, :], ww[...])
        wide[rows, :] = w
        active[rows, :] = smooth(w).astype(BF16)
        part[rows, :] = nn(active[rows, :], nw[...]).astype(BF16)
        for k in range(2):
            p = q * 2 + k

            @pl.when(p != m)
            def _send():
                mine = part.at[pl.ds(aligned(p * BLK, BLK), BLK)]
                remote(mine, rs1.at[m], row_s.at[0, p], row_r.at[0, m], {"mp": p}).start()

        return _

    lax.fori_loop(0, 4, forward, 0)

    def slopes_of(ref, n):
        def body(i, _):
            rows = pl.ds(aligned(i * 32, 32), 32)
            ref[rows, :] = smooth_slope(ref[rows, :])
            return _

        lax.fori_loop(0, n // 32, body, 0)

    def grid(shape, dim):
        return lax.broadcasted_iota(jnp.int32, shape, dim)

    def ones_where(condition):
        return condition.astype(F32).astype(BF16)

    for load in loads[3:]:
        load.wait()
    slot = slots[...].reshape(1, DP * DP)
    spread_out = ones_where(grid((DP * DP, R), 0) == d * DP + grid((DP * DP, R), 1) // PATCH)
    own_slot = nn(jnp.broadcast_to(slot, (16, DP * DP)).astype(F32).astype(BF16), spread_out)[0:1]
    goes = own_slot.astype(jnp.int32) // DP
    same_patch = lax.rem(grid((R, R), 0), PATCH) == lax.rem(grid((R, R), 1), PATCH)
    chosen = ones_where((goes == grid((R, R), 0) // PATCH) & same_patch)
    for t in range(3):
        late = (lags[t] - 1).astype(F32)
        stale = teachers[t][0].astype(F32) * (1.0 - late) + teachers[t][1].astype(F32) * late
        tsend[:, 256 * t : 256 * t + CB[t]] = nt(chosen, stale.astype(BF16)).astype(BF16)

    def images_of(j):
        return pl.ds(aligned(j * PATCH, PATCH), PATCH)

    def teach(i, _):
        j = lax.rem(d + i, DP)
        remote(tsend.at[images_of(j)], trecv.at[images_of(d)], tea_s.at[j], tea_r.at[d], {"dp": j}).start()
        return _

    lax.fori_loop(1, DP, teach, 0)
    trecv[images_of(d), :] = tsend[images_of(d), :]

    slopes_of(wide, R)
    for t in range(3):
        def head_block(i, _, t=t):
            at = aligned(i * 128, 128)
            headt[pl.ds(aligned(BASE[t] + at, 128), 128), :] = flipped(heads[t][:, pl.ds(at, 128)])
            return _

        lax.fori_loop(0, WIDTHS[t] // 128, head_block, 0)

    own_rows = pl.ds(aligned(m * BLK, BLK), BLK)

    def gathered(buffer, which, received):
        total = buffer[own_rows, :].astype(F32)
        for i in range(1, MP):
            p = mate(i)
            remote(received.at[p], received.at[p], row_s.at[which, p], row_r.at[which, p], {"mp": p}).wait_recv()
            total = total + received[p].astype(F32)
        return total

    def spread(buffer, which):
        def body(i, _):
            p = mate(i)
            remote(buffer.at[own_rows], buffer.at[own_rows], row_s.at[which, p], row_r.at[which, m], {"mp": p}).start()
            return _

        lax.fori_loop(1, MP, body, 0)

    def arrived(buffer, which):
        def body(i, _):
            p = mate(i)
            there = buffer.at[pl.ds(aligned(p * BLK, BLK), BLK)]
            remote(there, there, row_s.at[which, p], row_r.at[which, p], {"mp": p}).wait_recv()
            return _

        lax.fori_loop(1, MP, body, 0)

    hidden = tok[own_rows, :].astype(F32) + gathered(part, 0, rs1)
    centre = hidden - jnp.mean(hidden, axis=-1, keepdims=True)
    inv = lax.rsqrt(jnp.mean(centre * centre, axis=-1, keepdims=True) + 1e-06)
    normal[...] = centre * inv
    inverse[...] = jnp.broadcast_to(inv, (BLK, 128))
    final[own_rows, :] = (normal[...] * fg[...]).astype(BF16)
    spread(final, 1)

    def landed(i, _):
        j = lax.rem(d + i, DP)
        remote(tsend.at[images_of(j)], trecv.at[images_of(j)], tea_s.at[j], tea_r.at[j], {"dp": j}).wait_recv()
        return _

    lax.fori_loop(1, DP, landed, 0)

    holds = ones_where(slot == d * DP + grid((R, DP * DP), 0) // PATCH)
    group = ones_where(grid((R, DP * DP), 1) // DP == grid((R, DP * DP), 0) // PATCH)
    placing = jnp.where(same_patch, nt(group, holds), 0.0).astype(BF16)
    for t in range(3):
        block = flipped(trecv[:, 256 * t : 256 * t + CB[t]])
        tgt[OFF[t] : OFF[t] + CB[t], :] = nn(block, placing).astype(BF16)

    arrived(final, 1)

    pair, ring = m // 4, lax.rem(m, 4)

    def place(a, b):
        return a * 4 + lax.rem(b, 4)

    def channels(t, p):
        return pl.ds(aligned(BASE[t] + p * CB[t], 16), CB[t])

    def stu_copy(t, p, slot, k, to):
        there = rs2.at[slot, OFF[t] : OFF[t] + CB[t]]
        return remote(sp.at[channels(t, p)], there, stu_s.at[t, k], stu_r.at[t, slot], {"mp": to})

    def stu_got(t, slot):
        stu_copy(t, m, slot, slot, place(1 - pair, ring)).wait_recv()
        return rs2[slot, OFF[t] : OFF[t] + CB[t]].astype(F32)

    for t in range(3):
        units = slice(t * HB, (t + 1) * HB)
        b = nt(ai[t], final[...])
        before[units, :] = b
        lift[units, :] = smooth(b).astype(BF16)

        def student(p, t=t, units=units):
            rows = channels(t, p)
            sp[rows, :] = nn(headt[rows, :], lift[units, :]).astype(BF16)

        if t == 0:
            def over_pair(i, _, student=student):
                y = lax.rem(ring + i, 4)
                student(place(1 - pair, y))
                stu_copy(0, place(1 - pair, y), y, y, place(1 - pair, ring)).start()
                return _

            def kept(i, _, student=student):
                student(place(pair, ring + i))
                return _

            lax.fori_loop(0, 4, over_pair, 0)
            lax.fori_loop(0, 4, kept, 0)
        else:
            def over_ring(i, _, t=t, student=student):
                y, c = lax.rem(ring + 1 + i // 2, 4), lax.rem(i, 2)
                student(place(c, y))
                stu_copy(t, place(c, y), ring * 2 + c, y * 2 + c, place(pair, y)).start()
                return _

            def kept(i, _, student=student):
                student(place(i, ring))
                return _

            lax.fori_loop(0, 6, over_ring, 0)
            lax.fori_loop(0, 2, kept, 0)

    slopes_of(before, 3 * HB)

    def flip_all(src, dst):
        def body(i, _):
            at = aligned(i * 128, 128)
            dst[pl.ds(at, 128), :] = flipped(src[:, pl.ds(at, 128)])
            return _

        lax.fori_loop(0, D // 128, body, 0)

    flip_all(final, finalt)
    flip_all(first, firstt)

    def half_summed(t):
        mine = slice(OFF[t], OFF[t] + CB[t])
        if t == 0:
            def body(i, _):
                y = lax.rem(ring + i, 4)
                rows = channels(0, place(pair, y))
                sp[rows, :] = (sp[rows, :].astype(F32) + stu_got(0, y)).astype(BF16)
                stu_copy(0, place(pair, y), 4 + ring, 4 + y, place(pair, y)).start()
                return _

            lax.fori_loop(1, 4, body, 0)
            stu[mine, :] = sp[channels(0, m), :].astype(F32) + stu_got(0, ring)
        else:
            other = channels(t, place(1 - pair, ring))
            total = sp[other, :].astype(F32)
            for i in range(1, 4):
                total = total + stu_got(t, lax.rem(ring + i, 4) * 2 + 1 - pair)
            sp[other, :] = total.astype(BF16)
            stu_copy(t, place(1 - pair, ring), ring * 2, ring * 2, place(1 - pair, ring)).start()
            total = sp[channels(t, m), :].astype(F32)
            for i in range(1, 4):
                total = total + stu_got(t, lax.rem(ring + i, 4) * 2 + pair)
            stu[mine, :] = total

    def gather_student(t):
        mine = slice(OFF[t], OFF[t] + CB[t])
        if t == 0:
            for i in range(1, 4):
                stu[mine, :] += stu_got(0, 4 + lax.rem(ring + i, 4))
        else:
            stu[mine, :] += stu_got(t, ring * 2)
        y = stu[mine, :]
        f = tgt[mine, :].astype(F32)
        stats[t, 0:1, :] = jnp.sum(y * f, axis=0, keepdims=True)
        stats[t, 1:2, :] = jnp.sum(y * y, axis=0, keepdims=True)
        stats[t, 2:3, :] = jnp.sum(f * f, axis=0, keepdims=True)
        stats[t, 3:8, :] = jnp.zeros((5, R), F32)

        def send(i, _):
            p = mate(i)
            remote(stats.at[t], statr.at[t, m], sta_s.at[t, p], sta_r.at[t, m], {"mp": p}).start()
            return _

        lax.fori_loop(1, MP, send, 0)

    def slope(t):
        mine = slice(OFF[t], OFF[t] + CB[t])
        total = stats[t]
        for i in range(1, MP):
            p = mate(i)
            remote(stats.at[t], statr.at[t, p], sta_s.at[t, p], sta_r.at[t, p], {"mp": p}).wait_recv()
            total = total + statr[t, p]
        square_student = total[1:2] + 1e-06
        joint = lax.rsqrt(square_student * (total[2:3] + 1e-06))
        scale = total[0:1] * joint / square_student
        rows = pl.ds(aligned(BASE[t] + m * CB[t], 16), CB[t])
        slo[rows, :] = (scale * stu[mine, :] - joint * tgt[mine, :].astype(F32)).astype(BF16)

        pass_on(t, m, 0, place(pair, ring + 1))
        pass_on(t, m, 1, place(pair, ring + 3))
        pass_on(t, m, 2, place(1 - pair, ring))

    turn = (1, 3, 3)

    def slope_copy(t, owner, k, to):
        block = slo.at[pl.ds(aligned(BASE[t] + owner * CB[t], 16), CB[t])]
        return remote(block, block, slo_s.at[t, k], slo_r.at[t, owner], {"mp": to})

    def pass_on(t, owner, k, to):
        slope_copy(t, owner, k, to).start()

    def got(t, owner):
        slope_copy(t, owner, 0, owner).wait_recv()

    def first_relay(t):
        owner = place(pair, ring + 4 - turn[t])
        got(t, owner)
        pass_on(t, owner, 3, place(pair, ring + turn[t]))
        owner = place(1 - pair, ring)
        got(t, owner)
        pass_on(t, owner, 4, place(pair, ring + turn[t]))
        pass_on(t, owner, 5, place(pair, ring + 4 - turn[t]))

    def second_relay(t):
        owner = place(pair, ring + 2)
        got(t, owner)
        pass_on(t, owner, 6, place(1 - pair, ring))

    half_summed(1)
    half_summed(0)
    gather_student(1)
    half_summed(2)
    slope(1)
    gather_student(0)
    gather_student(2)
    first_relay(1)
    slope(0)
    slope(2)
    first_relay(0)
    second_relay(1)
    first_relay(2)
    second_relay(0)
    second_relay(2)

    for t in (1, 0, 2):
        got(t, place(pair, ring + turn[t]))
        got(t, place(1 - pair, ring + 4 - turn[t]))
        got(t, place(1 - pair, ring + turn[t]))
        got(t, place(1 - pair, ring + 2))
        units = slice(t * HB, (t + 1) * HB)
        back = nn(heads[t][...], slo[BASE[t] : BASE[t] + WIDTHS[t], :])
        inner[units, :] = (back * before[units, :]).astype(BF16)

    def up(i, _):
        q = lax.rem(m // 2 + 1 + i, 4)
        rows = pl.ds(aligned(q * 128, 128), 128)
        part2[rows, :] = nn(flipped(inner[:, rows]), ai[...].reshape(3 * HB, D)).astype(BF16)
        for k in range(2):
            p = q * 2 + k

            @pl.when(p != m)
            def _send():
                mine = part2.at[pl.ds(aligned(p * BLK, BLK), BLK)]
                remote(mine, rs3.at[m], row_s.at[2, p], row_r.at[2, m], {"mp": p}).start()

        return _

    lax.fori_loop(0, 4, up, 0)

    def to_partner(which, send, received):
        def body(k, _):
            j = k * 2 + (1 - core)
            remote(send.at[j], received.at[k], cor_s.at[which, k], cor_r.at[which, k], {"dp": partner}).start()
            return _

        lax.fori_loop(0, 8, body, 0)

    def onward(which, send, received, mid, last):
        def body(i, _):
            k = lax.rem(half + i, 8)
            remote(send.at[k], received.at[k], cor_s.at[which, k], cor_r.at[which, k], {"dp": partner}).wait_recv()
            mid[k] = (send[k * 2 + core].astype(F32) + received[k].astype(F32)).astype(BF16)

            @pl.when(k != half)
            def _send():
                remote(mid.at[k], last.at[half], dp_s.at[which, k], dp_r.at[which, half], {"dp": k * 2 + core}).start()

            return _

        lax.fori_loop(1, 9, body, 0)

    def reduced(which, mid, last, out):
        out[...] = mid[half].astype(F32)

        def body(i, _):
            k = lax.rem(half + i, 8)
            remote(mid.at[k], last.at[k], dp_s.at[which, k], dp_r.at[which, k], {"dp": k * 2 + core}).wait_recv()
            out[...] += last[k].astype(F32)
            return _

        lax.fori_loop(1, 8, body, 0)

    def pieces(dst, j, value):
        for k in range(4):
            dst[j * 4 + k] = value[k * DB : (k + 1) * DB].astype(BF16)

    side, level = half // 4, lax.rem(half, 4)

    def chip(a, b):
        return {"dp": (a * 4 + b) * 2 + core}

    def along(which, mid, last, k, slot, send, to):
        return remote(mid.at[k], last.at[slot], dp_s.at[which, send], dp_r.at[which, slot], to)

    def along_z(which, send, received, mid, last):
        def body(i, _):
            z, a = lax.rem(level + 1 + i // 2, 4), lax.rem(i, 2)
            k = a * 4 + z
            remote(send.at[k], received.at[k], cor_s.at[which, k], cor_r.at[which, k], {"dp": partner}).wait_recv()
            mid[k] = (send[k * 2 + core].astype(F32) + received[k].astype(F32)).astype(BF16)

            @pl.when(z != level)
            def _send():
                along(which, mid, last, k, level * 2 + a, z * 2 + a, chip(side, z)).start()

            return _

        lax.fori_loop(0, 8, body, 0)

    def z_sum(which, mid, last, a):
        total = mid[a * 4 + level].astype(F32)
        for i in range(1, 4):
            z = lax.rem(level + i, 4)
            along(which, mid, last, 0, z * 2 + a, 0, chip(side, z)).wait_recv()
            total = total + last[z * 2 + a].astype(F32)
        return total

    def over_x(which, mid, last):
        k = (1 - side) * 4 + level
        mid[k] = z_sum(which, mid, last, 1 - side).astype(BF16)
        along(which, mid, last, k, level * 2, level * 2, chip(1 - side, level)).start()

    def reduced_zx(which, mid, last, out):
        total = z_sum(which, mid, last, side)
        along(which, mid, last, 0, level * 2, 0, chip(1 - side, level)).wait_recv()
        out[...] = total + last[level * 2].astype(F32)

    for t in range(3):
        def head_grad(i, _, t=t):
            n = (384, 384, 640)[t]
            at = aligned(i * n, 128)
            rows = pl.ds(aligned(BASE[t] + at, 128), n)
            hf32[pl.ds(at, n), :] = nt(slo[rows, :], lift[t * HB : (t + 1) * HB, :])
            return _

        lax.fori_loop(0, WIDTHS[t] // (384, 384, 640)[t], head_grad, 0)

        def head_piece(j, _, t=t):
            rows = pl.ds(aligned(j * PB[t], 8), PB[t])
            hsend[j, HOFF[t] : HOFF[t] + PB[t], :] = hf32[rows, :].astype(BF16)
            return _

        lax.fori_loop(0, DP, head_piece, 0)
    to_partner(0, hsend, hcore)

    def adaptor_grad(j, _):
        pieces(asend, j, nt(finalt[pl.ds(aligned(j * 4 * DB, 16), 4 * DB), :], inner[...]))
        return _

    lax.fori_loop(0, DP // 4, adaptor_grad, 0)
    to_partner(1, asend, acore)
    along_z(0, hsend, hcore, hmid, hrecv)
    along_z(1, asend, acore, amid, arecv)

    upstream = gathered(part2, 2, rs3)
    scaled = upstream * fg[...]
    hat = normal[...]
    through = inverse[:, 0:1] * (
        scaled
        - jnp.mean(scaled, axis=-1, keepdims=True)
        - hat * jnp.mean(scaled * hat, axis=-1, keepdims=True)
    )
    thr[own_rows, :] = through.astype(BF16)
    spread(thr, 3)
    over_x(0, hmid, hrecv)
    over_x(1, amid, arecv)
    arrived(thr, 3)

    flip_all(thr, finalt)

    def narrow_grad(j, _):
        pieces(nsend, j, nn(finalt[pl.ds(aligned(j * 4 * DB, 16), 4 * DB), :], active[...]))
        return _

    lax.fori_loop(0, DP // 4, narrow_grad, 0)
    to_partner(2, nsend, ncore)
    def backward(i, _):
        rows = pl.ds(aligned(i * 128, 128), 128)
        active[rows, :] = (nt(thr[rows, :], nw[...]) * wide[rows, :]).astype(BF16)
        return _

    lax.fori_loop(0, 4, backward, 0)
    onward(2, nsend, ncore, nmid, nrecv)

    def widen_grad(j, _):
        pieces(wsend, j, nn(firstt[pl.ds(aligned(j * 4 * DB, 16), 4 * DB), :], active[...]))
        return _

    lax.fori_loop(0, DP // 4, widen_grad, 0)
    to_partner(3, wsend, wcore)
    onward(3, wsend, wcore, wmid, wrecv)
    reduced_zx(0, hmid, hrecv, hacc)
    out_d[...] = hacc[0:96, :].T
    out_g[...] = hacc[96:168, :]
    out_s[...] = hacc[176:256, :].T
    reduced_zx(1, amid, arecv, aacc)
    for t in range(3):
        out_a[t] = aacc[:, t * HB : (t + 1) * HB]
    reduced(2, nmid, nrecv, out_n)
    reduced(3, wmid, wrecv, out_w)

    def sent_dp(i, _):
        j = lax.rem(d + i, DP)
        remote(tsend.at[images_of(j)], trecv.at[images_of(d)], tea_s.at[j], tea_r.at[d], {"dp": j}).wait_send()
        return _

    lax.fori_loop(1, DP, sent_dp, 0)

    def sent_mp(i, _):
        p = mate(i)
        where = {"mp": p}
        for which, (src, dst) in enumerate(((part, rs1), (final, rs1), (part2, rs3), (thr, rs3))):
            remote(src.at[own_rows], dst.at[m], row_s.at[which, p], row_r.at[which, m], where).wait_send()
        for t in range(3):
            remote(stats.at[t], statr.at[t, m], sta_s.at[t, p], sta_r.at[t, m], where).wait_send()
        return _

    lax.fori_loop(1, MP, sent_mp, 0)
    for t in range(3):
        for k in range(7):
            slope_copy(t, m, k, place(pair, ring + 1)).wait_send()
        for i in range(1, 4):
            y = lax.rem(ring + i, 4)
            if t == 0:
                stu_copy(0, m, y, y, place(1 - pair, ring)).wait_send()
                stu_copy(0, m, y, 4 + y, place(1 - pair, ring)).wait_send()
            else:
                stu_copy(t, m, y, y * 2, place(1 - pair, ring)).wait_send()
                stu_copy(t, m, y, y * 2 + 1, place(1 - pair, ring)).wait_send()
        k = ring if t == 0 else ring * 2
        stu_copy(t, m, k, k, place(1 - pair, ring)).wait_send()
    reductions = (
        (hsend, hcore, hmid, hrecv),
        (asend, acore, amid, arecv),
        (nsend, ncore, nmid, nrecv),
        (wsend, wcore, wmid, wrecv),
    )

    def sent_core(k, _):
        for which, (send, received, mid, last) in enumerate(reductions):
            remote(send.at[k], received.at[k], cor_s.at[which, k], cor_r.at[which, k], {"dp": partner}).wait_send()
        return _

    lax.fori_loop(0, 8, sent_core, 0)

    def sent_chip(i, _):
        k = lax.rem(half + i, 8)
        for which, (send, received, mid, last) in list(enumerate(reductions))[2:]:
            remote(mid.at[k], last.at[half], dp_s.at[which, k], dp_r.at[which, half], {"dp": k * 2 + core}).wait_send()
        return _

    lax.fori_loop(1, 8, sent_chip, 0)
    for which, (send, received, mid, last) in list(enumerate(reductions))[:2]:
        for i in range(1, 4):
            z = lax.rem(level + i, 4)
            for a in range(2):
                along(which, mid, last, 0, 0, z * 2 + a, chip(1 - side, level)).wait_send()
        along(which, mid, last, 0, 0, level * 2, chip(1 - side, level)).wait_send()


def local(
    tokens, norm_gain, widen_weight, narrow_weight, final_gain, adaptor_in,
    head_dino, head_siglip, head_sam, teacher_dino, teacher_siglip, teacher_sam,
    step_lags, owner_slot,
):
    vmem = pl.BlockSpec(memory_space=pltpu.VMEM)

    def reduction(rows, columns):
        return [
            pltpu.VMEM((DP, rows, columns), BF16),
            pltpu.VMEM((8, rows, columns), BF16),
            pltpu.VMEM((8, rows, columns), BF16),
            pltpu.VMEM((8, rows, columns), BF16),
        ]

    dma = pltpu.SemaphoreType.DMA
    arrays = (
        tokens, widen_weight, narrow_weight,
        teacher_dino.transpose(0, 2, 1), teacher_siglip.transpose(0, 2, 1), teacher_sam.transpose(0, 2, 1),
        adaptor_in.transpose(0, 2, 1), head_dino, head_siglip, head_sam,
    )
    w, n, a, dino, siglip, sam = pl.pallas_call(
        kernel,
        out_shape=(
            jax.ShapeDtypeStruct((DB, FB), F32),
            jax.ShapeDtypeStruct((DB, FB), F32),
            jax.ShapeDtypeStruct((3, DB, HB), F32),
            jax.ShapeDtypeStruct((HB, PB[0]), F32),
            jax.ShapeDtypeStruct((PB[1], HB), F32),
            jax.ShapeDtypeStruct((HB, PB[2]), F32),
        ),
        in_specs=[pl.BlockSpec(memory_space=pltpu.SMEM)] + [vmem] * 3 + [pl.BlockSpec(memory_space=pl.ANY)] * 10,
        out_specs=(vmem,) * 6,
        scratch_shapes=[
            *[pltpu.VMEM(array.shape, array.dtype) for array in arrays],
            dma((len(arrays),)),
            pltpu.VMEM((R, D), BF16),
            pltpu.VMEM((R, FB), F32),
            pltpu.VMEM((R, FB), BF16),
            pltpu.VMEM((R, D), BF16),
            pltpu.VMEM((MP, BLK, D), BF16),
            pltpu.VMEM((R, D), BF16),
            pltpu.VMEM((BLK, D), F32),
            pltpu.VMEM((BLK, 128), F32),
            pltpu.VMEM((CH, HB), BF16),
            pltpu.VMEM((3 * HB, R), F32),
            pltpu.VMEM((3 * HB, R), BF16),
            pltpu.VMEM((CH, R), BF16),
            pltpu.VMEM((MP, CBS, R), BF16),
            pltpu.VMEM((CBS, R), F32),
            pltpu.VMEM((R, 768), BF16),
            pltpu.VMEM((R, 768), BF16),
            pltpu.VMEM((CBS, R), BF16),
            pltpu.VMEM((3, 8, R), F32),
            pltpu.VMEM((3, MP, 8, R), F32),
            pltpu.VMEM((CH, R), BF16),
            pltpu.VMEM((3 * HB, R), BF16),
            pltpu.VMEM((R, D), BF16),
            pltpu.VMEM((MP, BLK, D), BF16),
            pltpu.VMEM((R, D), BF16),
            pltpu.VMEM((D, R), BF16),
            pltpu.VMEM((D, R), BF16),
            pltpu.VMEM((1536, HB), F32),
            pltpu.VMEM((256, HB), F32),
            pltpu.VMEM((DB, 3 * HB), F32),
            *reduction(256, HB),
            *reduction(DB, 3 * HB),
            *reduction(DB, FB),
            *reduction(DB, FB),
            dma((4, MP)), dma((4, MP)),
            dma((DP,)), dma((DP,)),
            dma((3, MP)), dma((3, MP)),
            dma((3, MP)), dma((3, MP)),
            dma((3, MP)), dma((3, MP)),
            dma((4, 8)), dma((4, 8)),
            dma((4, 8)), dma((4, 8)),
        ],
        compiler_params=pltpu.CompilerParams(
            collective_id=0, has_side_effects=True, vmem_limit_bytes=66_000_000
        ),
        name="step",
    )(
        step_lags, owner_slot[None], norm_gain[None], final_gain[None], *arrays
    )
    return w.T, n.T, a, dino, siglip.T, sam


def solution(mesh):
    placed = (
        P("dp", None),
        P(),
        P(None, "mp"),
        P("mp", None),
        P(),
        P(None, None, "mp"),
        P("mp", None),
        P("mp", None),
        P("mp", None),
        P(None, "dp", "mp"),
        P(None, "dp", "mp"),
        P(None, "dp", "mp"),
        P(),
        P(),
    )
    return jax.shard_map(
        local,
        mesh=mesh,
        in_specs=placed,
        out_specs=(
            P("mp", "dp"),
            P("mp", "dp"),
            P(None, "dp", "mp"),
            P("mp", "dp"),
            P("mp", "dp"),
            P("mp", "dp"),
        ),
        check_vma=False,
    )
```
